32 devices in a mesh: orb: 8 (over z, y), pair: 4 (over x, core).
Axes of the slice: x: 2, y: 2, z: 4, core: 2. Of those that a mesh axis runs over, the one named last changes fastest.
Arguments:
- orbitals: float32 [16, 32, 1024], P('orb'), may hold values from -6 to 6
- send_index: int32 [8, 4, 8], P('orb', 'pair'), may hold values from -1 to 1, as said below
- pair_left: int32 [8, 4, 8], P('orb', 'pair'), may hold values from -1 to 1, as said below
- pair_offset: int32 [8, 4, 8], P('orb', 'pair'), may hold values from -8 to 8
Outputs:
- exchange_field: float32 [16, 32, 1024], P('orb', 'pair')
The draws below stay inside these ranges and needn't reach their ends.
Inputs may be any that keep to these rules, and one draw needn't show every extreme that they name: `send_index`: -1 marks an empty route. Toward some orb index, drawn from the seed, every route from every device is live. pair_left[d, p, s + c] is -1 exactly when send_index[s, p, d + c] is -1.
All inputs are finite; a program needn't handle non-finite values.
Results may differ from the reference program's by a relative error of at most 0.0075.
Values may be sent and summed in bfloat16 or wider, within the bound.
A program may use at most 128 MiB of HBM per device.

```python
import jax
import jax.numpy as jnp
from jax import lax

B = 32
ORB_DEV = 2
CAP = 1
SWEEPS = 2
ORBITALS = 16
N_ORB = 8
N_PAIR = 4


def route_mask(key):
    base = jax.random.fold_in(key, 7)
    level_key, full_key, route_key = jax.random.split(base, 3)
    levels = 2 ** jax.random.randint(level_key, (N_PAIR, N_ORB), 0, 4)
    busiest = jax.random.randint(full_key, (), 0, N_ORB)
    levels = jnp.where(jnp.arange(N_ORB)[None, :] == busiest, 8, levels)
    draws = jax.random.randint(route_key, (N_ORB, N_PAIR, N_ORB, CAP), 0, 8)
    return draws < levels[None, :, :, None]


def draw_send_index(key, part):
    live_mask = route_mask(key)
    chosen = jax.random.randint(jax.random.fold_in(key, 11), (N_ORB, N_PAIR, N_ORB, CAP), 0, ORB_DEV)
    return jnp.where(live_mask, chosen, -1).reshape(N_ORB, N_PAIR, N_ORB * CAP).astype(jnp.int32)


def draw_pair_left(key, part):
    live_mask = jnp.transpose(route_mask(key), (2, 1, 0, 3))
    chosen = jax.random.randint(jax.random.fold_in(key, 13), (N_ORB, N_PAIR, N_ORB, CAP), 0, ORB_DEV)
    return jnp.where(live_mask, chosen, -1).reshape(N_ORB, N_PAIR, N_ORB * CAP).astype(jnp.int32)


def touch_ends(array, key, smallest, high):
    place = [jax.random.randint(jax.random.fold_in(key, axis), (), 0, length) for axis, length in enumerate(array.shape)]
    widest = array.shape.index(max(array.shape))
    next_to = place[:widest] + [(place[widest] + 1) % array.shape[widest]] + place[widest + 1:]
    return array.at[tuple(place)].set(smallest).at[tuple(next_to)].set(high)


def shard_levels(own_key, extent, pieces, smallest, top_value):
    def one(dim, shards_of):
        steps = jax.random.uniform(jax.random.fold_in(jax.random.fold_in(own_key, 6), dim), (shards_of,), jnp.float32, smallest / len(pieces), top_value / len(pieces))
        return jnp.repeat(jnp.exp(steps), extent[dim] // shards_of).reshape((-1,) + (1,) * (len(extent) - dim - 1))

    gain = one(*pieces[0])
    for cut in pieces[1:]:
        gain = gain * one(*cut)
    return gain


def gaussian(stream_key, extent, scale, limit, shards=(), kind=jnp.bfloat16):
    factor_of = shard_levels(stream_key, extent, shards, -0.22, 0.18) if shards else 1.0
    result = jax.random.normal(stream_key, extent, jnp.float32) * scale * factor_of
    return jnp.minimum(jnp.maximum(result, -limit), limit).astype(kind)


def setup_inputs(seed: int = 0) -> dict:
    key_list = jax.random.split(jax.random.key(seed), 5)
    orbitals = gaussian(key_list[0], (ORBITALS, B, B * B), 1.0, 6.0, ((0, 8),), jnp.float32)
    send_index = draw_send_index(jax.random.fold_in(key_list[4], 71), 0)
    pair_left = draw_pair_left(jax.random.fold_in(key_list[4], 71), 0)
    pair_offset = touch_ends(jax.random.randint(key_list[3], (N_ORB, N_PAIR, N_ORB * CAP), -(B // 4), B // 4 + 1), jax.random.fold_in(key_list[3], 1), -(B // 4), (B // 4 + 1) - 1).astype(jnp.int32)
    return dict(orbitals=orbitals, send_index=send_index, pair_left=pair_left, pair_offset=pair_offset)


def neighbours(field):
    box_side = field.shape[1]
    plane = field.shape[2]
    edge_x = jnp.zeros_like(field[:, :1])
    summed = jnp.concatenate([field[:, 1:], edge_x], 1) + jnp.concatenate([edge_x, field[:, :-1]], 1)
    edge_y = jnp.zeros_like(field[:, :, :box_side])
    summed = summed + jnp.concatenate([field[:, :, box_side:], edge_y], 2) + jnp.concatenate([edge_y, field[:, :, :-box_side]], 2)
    edge_z = jnp.zeros_like(field[:, :, :1])
    column = lax.broadcasted_iota(jnp.int32, (1, 1, plane), 2) % box_side
    upper = jnp.where(column < box_side - 1, jnp.concatenate([field[:, :, 1:], edge_z], 2), 0.0)
    lower = jnp.where(column > 0, jnp.concatenate([edge_z, field[:, :, :-1]], 2), 0.0)
    return summed + upper + lower


def pair_work(left, right, offsets):
    box_side = left.shape[1]
    positions = jnp.arange(box_side, dtype=jnp.int32)
    forward = (positions[None, None, :] == positions[None, :, None] - offsets[:, None, None]).astype(jnp.float32)
    shifted_right = jnp.einsum("rxw,rwc->rxc", forward, right.astype(jnp.float32), precision=lax.Precision.HIGHEST)
    left_wide = left.astype(jnp.float32)
    density = left_wide * shifted_right
    potential = jnp.zeros_like(density)
    for sweep_number in range(SWEEPS):
        potential = (neighbours(potential) + density) / 6.0
    to_left = (potential * shifted_right).astype(jnp.bfloat16)
    backward = (positions[None, None, :] == positions[None, :, None] + offsets[:, None, None]).astype(jnp.float32)
    to_right = jnp.einsum("rxw,rwc->rxc", backward, potential * left_wide, precision=lax.Precision.HIGHEST)
    return to_left, to_right.astype(jnp.bfloat16)


def reference(orbitals, send_index, pair_left, pair_offset):
    rounded = orbitals.astype(jnp.bfloat16)
    slot_count = N_ORB * CAP
    source = (jnp.arange(slot_count, dtype=jnp.int32) // CAP).astype(jnp.int32)
    total = jnp.zeros(orbitals.shape, jnp.float32)
    for pair_number in range(N_PAIR):
        def visit(accumulated, owner_index):
            zero = (owner_index * 0).astype(jnp.int32)
            pair_index = (zero + pair_number).astype(jnp.int32)
            left_rows = lax.dynamic_slice(pair_left, (owner_index, pair_index, zero), (1, 1, slot_count)).reshape(slot_count)
            offsets = lax.dynamic_slice(pair_offset, (owner_index, pair_index, zero), (1, 1, slot_count)).reshape(slot_count)
            send_rows = lax.dynamic_slice(send_index, (zero, pair_index, (owner_index * CAP).astype(jnp.int32)), (N_ORB, 1, CAP)).reshape(slot_count)
            live_mask = left_rows >= 0
            left_id = jnp.where(live_mask, owner_index * ORB_DEV + left_rows, 0).astype(jnp.int32)
            right_id = jnp.where(live_mask, source * ORB_DEV + send_rows, 0).astype(jnp.int32)
            left = jnp.where(live_mask[:, None, None], rounded[left_id], jnp.zeros((), jnp.bfloat16))
            right = jnp.where(live_mask[:, None, None], rounded[right_id], jnp.zeros((), jnp.bfloat16))
            to_left, to_right = pair_work(left, right, offsets)
            accumulated = accumulated.at[left_id].add(jnp.where(live_mask[:, None, None], to_left.astype(jnp.float32), 0.0))
            accumulated = accumulated.at[right_id].add(jnp.where(live_mask[:, None, None], to_right.astype(jnp.float32), 0.0))
            return accumulated, None

        start = jnp.zeros(orbitals.shape, jnp.float32)
        partial_value, unused = lax.scan(visit, start, jnp.arange(N_ORB, dtype=jnp.int32))
        partial_rounded = lax.optimization_barrier(partial_value.astype(jnp.bfloat16))
        total = total + partial_rounded.astype(jnp.float32)
    return -0.25 * total
```

```python
import functools

import jax
import jax.numpy as jnp
from jax import lax
from jax.experimental import pallas as pl
from jax.experimental.pallas import tpu as pltpu
from jax.sharding import PartitionSpec as P

LANES = 128
DEAD = -10000.0
f32, bf16 = jnp.float32, jnp.bfloat16


def repeat(start, stop, body):
    if stop - start <= 8:
        for k in range(start, stop):
            body(k)
    else:
        lax.fori_loop(start, stop, lambda k, c: (body(k), c)[1], 0)


def kernel(
    n_orb,
    n_pair,
    orb_ref,
    send_ref,
    left_ref,
    off_ref,
    out_ref,
    slab,
    edges,
    raw,
    boxes,
    sums,
    tab_pair,
    tab_orb,
    out_d,
    load_sem,
    send_a,
    recv_a,
    send_p,
    recv_p,
    send_i,
    recv_i,
    send_d,
    recv_d,
):
    owned, box_side, plane = orb_ref.shape
    groups = plane // n_pair // LANES
    width = groups * LANES
    own_rows = box_side // n_pair
    slots = send_ref.shape[2]
    side = owned * box_side
    me = lax.axis_index("orb")
    mine = lax.axis_index("pair")
    barrier = pltpu.get_barrier_semaphore()

    def other_orb(k):
        return lax.rem(me + k, n_orb)

    def other_pair(k):
        return lax.rem(mine + k, n_pair)

    first = mine * groups
    below = jnp.maximum(first - 1, 0)
    above = jnp.minimum(first + groups, groups * n_pair - 1)

    def lanes_of(c, n):
        return pl.ds(pl.multiple_of(c * LANES, LANES), n * LANES)

    loads = [
        pltpu.make_async_copy(send_ref, raw.at[0], load_sem.at[0]),
        pltpu.make_async_copy(left_ref, raw.at[1], load_sem.at[1]),
        pltpu.make_async_copy(off_ref, raw.at[2], load_sem.at[2]),
        pltpu.make_async_copy(orb_ref.at[:, :, lanes_of(first, groups)], slab, load_sem.at[3]),
        pltpu.make_async_copy(orb_ref.at[:, :, lanes_of(below, 1)], edges.at[0], load_sem.at[4]),
        pltpu.make_async_copy(orb_ref.at[:, :, lanes_of(above, 1)], edges.at[1], load_sem.at[5]),
    ]
    for load in loads:
        load.start()

    repeat(1, n_orb, lambda k: pl.semaphore_signal(barrier, inc=1, device_id={"orb": other_orb(k)}))
    repeat(1, n_pair, lambda k: pl.semaphore_signal(barrier, inc=1, device_id={"pair": other_pair(k)}))

    for load in loads[:3]:
        load.wait()
    sent, left, off = (raw[i, 0].astype(f32) for i in range(3))
    dead = left < 0
    tab_pair[mine, 0:1] = box_side * 2 * sent
    tab_pair[mine, 1:2] = jnp.where(dead, DEAD, box_side * 2 * left - off)
    tab_pair[mine, 2:3] = jnp.where(dead, DEAD, 2 * box_side * owned * left + off)
    tab_pair[mine, 3:4] = 2 * box_side * owned * sent

    for load in loads[3:]:
        load.wait()
    lane = lax.broadcasted_iota(jnp.int32, (box_side, LANES), 1)
    row = lax.broadcasted_iota(jnp.int32, (box_side, LANES), 0)
    has_below = lane + jnp.where(mine > 0, 0, LANES) < box_side
    has_above = lane - jnp.where(mine < n_pair - 1, 0, LANES) >= LANES - box_side
    halos = []
    for b in range(owned):
        for g in range(groups):
            boxes[me, b * groups + g] = slab[b, :, g * LANES : (g + 1) * LANES].astype(bf16)
        halo = jnp.where(has_below, pltpu.roll(edges[0, b], box_side, 1), 0.0)
        halo = jnp.where(has_above, pltpu.roll(edges[1, b], LANES - box_side, 1), halo)
        halos.append(halo if b == 0 else pltpu.roll(halo, b * 2 * box_side, 1))
    boxes[me, owned * groups] = functools.reduce(jnp.add, halos).astype(bf16)

    pl.semaphore_wait(barrier, n_orb - 1 + n_pair - 1)

    fold = 2 if n_orb % 2 == 0 else 1
    lines = n_orb // fold
    high, low = me // fold, lax.rem(me, fold)

    def peer(k, over):
        return lax.rem(high + k + lines, lines) * fold + lax.rem(low + over, fold)

    def copy_a(block, o):
        return pltpu.make_async_remote_copy(
            src_ref=boxes.at[block],
            dst_ref=boxes.at[block],
            send_sem=send_a.at[o if block is me else n_orb + block],
            recv_sem=recv_a.at[block],
            device_id={"orb": o},
        )

    def copy_p(q, at):
        return pltpu.make_async_remote_copy(
            src_ref=tab_pair.at[mine],
            dst_ref=tab_pair.at[at],
            send_sem=send_p.at[q],
            recv_sem=recv_p.at[at],
            device_id={"pair": q},
        )

    def copy_i(o, at):
        return pltpu.make_async_remote_copy(
            src_ref=tab_orb.at[me],
            dst_ref=tab_orb.at[at],
            send_sem=send_i.at[o],
            recv_sem=recv_i.at[at],
            device_id={"orb": o},
        )

    def copy_d(q, at):
        return pltpu.make_async_remote_copy(
            src_ref=out_d.at[q],
            dst_ref=out_ref.at[:, pl.ds(pl.multiple_of(at * width, LANES), width)],
            send_sem=send_d.at[q],
            recv_sem=recv_d.at[at],
            device_id={"pair": q},
        )

    if fold > 1:
        copy_a(me, peer(0, 1)).start()
    repeat(1, lines, lambda k: copy_a(me, peer(k, 0)).start())
    repeat(1, n_pair, lambda k: copy_p(other_pair(k), mine).start())

    inner = lane % box_side < box_side - 1
    near = lane < LANES - box_side
    not_last = row < box_side - 1
    not_first = row > 0

    def up(v):
        return jnp.where(not_last, pltpu.roll(v, box_side - 1, 0), 0.0)

    def next_y(own, following):
        return jnp.where(near, pltpu.roll(own, LANES - box_side, 1), following)

    def pieces(s, m):
        own = [boxes[s, m * groups + g].astype(f32) for g in range(groups)]
        halo = boxes[s, owned * groups].astype(f32)
        if m:
            halo = pltpu.roll(halo, LANES - m * 2 * box_side, 1)
        rolled = [pltpu.roll(v, LANES - box_side, 1) for v in own]
        after = [
            jnp.where(near, rolled[g], rolled[g + 1] if g + 1 < groups else halo)
            for g in range(groups)
        ]
        return own, after, halo

    def products(s):
        rows = []
        for m in range(owned):
            own, after, halo = pieces(s, m)
            parts = [v * v for v in own]
            parts += [v * up(v) for v in own]
            parts += [jnp.where(inner, v * pltpu.roll(v, LANES - 1, 1), 0.0) for v in own]
            parts += [v * w for v, w in zip(own, after)]
            parts += [halo * own[0]]
            rows.append(jnp.concatenate([p.astype(bf16) for p in parts], axis=1))
        return jnp.concatenate(rows, axis=0)

    at_row = lax.broadcasted_iota(jnp.int32, (side, side), 0)
    at_col = lax.broadcasted_iota(jnp.int32, (side, side), 1)
    key = at_row % box_side - at_col % box_side
    key = key + 2 * box_side * (at_col // box_side) + 2 * box_side * owned * (at_row // box_side)
    key = key.astype(f32)
    slot = lax.broadcasted_iota(jnp.int32, (2 * n_pair, slots), 1)

    def counts(s, own_tab):
        codes = jnp.where(slot == me, tab_orb[s], 0.0) + jnp.where(slot == s, own_tab, 0.0)
        codes = jnp.sum(codes, axis=1, keepdims=True)
        total = jnp.zeros((side, side), f32)
        for u in range(2 * n_pair):
            total = total + jnp.where(key == codes[u : u + 1, :], 1.0, 0.0)
        return total.astype(bf16)

    def multiply(band, prods):
        return jnp.dot(band, prods, preferred_element_type=f32)

    prods = products(me)
    repeat(1, n_pair, lambda k: copy_p(other_pair(k), other_pair(k)).wait_recv())
    tab_orb[me] = jnp.concatenate(
        [tab_pair[p, r : r + 1] for r in (0, 1) for p in range(n_pair)], axis=0
    )
    own_tab = jnp.concatenate(
        [tab_pair[p, r : r + 1] for r in (2, 3) for p in range(n_pair)], axis=0
    )
    repeat(1, n_orb, lambda k: copy_i(other_orb(k), me).start())
    sums[...] = multiply(counts(me, own_tab), prods)

    def process(s):
        prods = products(s)
        copy_i(s, s).wait_recv()
        sums[...] = sums[...] + multiply(counts(s, own_tab), prods)

    def on_line(k):
        s = peer(-k, 0)
        copy_a(s, s).wait_recv()
        if fold > 1:
            copy_a(s, peer(0, 1)).start()
        process(s)

    def across(k):
        s = peer(-k, 1)
        copy_a(s, s).wait_recv()
        process(s)

    repeat(1, lines, on_line)
    if fold > 1:
        repeat(0, lines, across)

    scale = -0.25 / 36.0
    fields = {}
    for k in range(owned):
        own, after, halo = pieces(me, k)

        def part(i):
            return sums[k * box_side : (k + 1) * box_side, i * LANES : (i + 1) * LANES]

        flux = [pltpu.roll(part(3 * groups + g) * own[g], box_side, 1) for g in range(groups)]
        flux_below = part(4 * groups) * halo
        for g in range(groups):
            here = own[g]
            value = 6.0 * (part(g) * here)
            c_x = part(groups + g)
            value = value + c_x * up(here)
            value = value + jnp.where(not_first, pltpu.roll(c_x * here, 1, 0), 0.0)
            c_z = part(2 * groups + g)
            value = value + c_z * pltpu.roll(here, LANES - 1, 1) + pltpu.roll(c_z * here, 1, 1)
            value = value + part(3 * groups + g) * after[g]
            value = value + jnp.where(lane >= box_side, flux[g], flux[g - 1] if g else flux_below)
            fields[k, g] = value * scale

    for q in range(n_pair):
        for g in range(groups):
            at = slice(q * own_rows, (q + 1) * own_rows)
            rows = jnp.concatenate([fields[k, g][at] for k in range(owned)], axis=0)
            out_d[q, :, g * LANES : (g + 1) * LANES] = rows.astype(bf16)

    repeat(1, n_pair, lambda k: copy_d(other_pair(k), mine).start())
    keep = pltpu.make_async_copy(
        out_d.at[mine],
        out_ref.at[:, pl.ds(pl.multiple_of(mine * width, LANES), width)],
        load_sem.at[0],
    )
    keep.start()
    repeat(1, n_pair, lambda k: copy_d(other_pair(k), other_pair(k)).wait_recv())
    keep.wait()

    if fold > 1:
        copy_a(me, peer(0, 1)).wait_send()
        repeat(1, lines, lambda k: copy_a(peer(-k, 0), peer(0, 1)).wait_send())
    repeat(1, lines, lambda k: copy_a(me, peer(k, 0)).wait_send())
    repeat(1, n_orb, lambda k: copy_i(other_orb(k), me).wait_send())
    repeat(1, n_pair, lambda k: copy_p(other_pair(k), mine).wait_send())
    repeat(1, n_pair, lambda k: copy_d(other_pair(k), mine).wait_send())


def local(n_orb, n_pair, orbitals, send_index, pair_left, pair_offset):
    owned, box_side, plane = orbitals.shape
    slots = send_index.shape[2]
    groups = plane // n_pair // LANES
    own_rows = box_side // n_pair
    assert owned * 2 * box_side == LANES and slots == n_orb
    hbm = pl.BlockSpec(memory_space=pl.ANY)
    dma = pltpu.SemaphoreType.DMA
    field = pl.pallas_call(
        functools.partial(kernel, n_orb, n_pair),
        out_shape=jax.ShapeDtypeStruct((owned * own_rows, plane), bf16),
        in_specs=[hbm] * 4,
        out_specs=hbm,
        scratch_shapes=[
            pltpu.VMEM((owned, box_side, groups * LANES), f32),
            pltpu.VMEM((2, owned, box_side, LANES), f32),
            pltpu.VMEM((3, 1, 1, slots), jnp.int32),
            pltpu.VMEM((n_orb, owned * groups + 1, box_side, LANES), bf16),
            pltpu.VMEM((owned * box_side, (4 * groups + 1) * LANES), f32),
            pltpu.VMEM((n_pair, 4, slots), f32),
            pltpu.VMEM((n_orb, 2 * n_pair, slots), f32),
            pltpu.VMEM((n_pair, owned * own_rows, groups * LANES), bf16),
            dma((6,)),
            dma((2 * n_orb,)),
            dma((n_orb,)),
            dma((n_pair,)),
            dma((n_pair,)),
            dma((n_orb,)),
            dma((n_orb,)),
            dma((n_pair,)),
            dma((n_pair,)),
        ],
        compiler_params=pltpu.CompilerParams(
            collective_id=0, has_side_effects=True, vmem_limit_bytes=16 << 20
        ),
        name="exchange",
    )(orbitals, send_index, pair_left, pair_offset)
    return field.astype(f32).reshape(owned, own_rows, plane)


def solution(mesh):
    n_orb, n_pair = mesh.shape["orb"], mesh.shape["pair"]
    return jax.shard_map(
        functools.partial(local, n_orb, n_pair),
        mesh=mesh,
        in_specs=(
            P("orb", None, None),
            P("orb", "pair", None),
            P("orb", "pair", None),
            P("orb", "pair", None),
        ),
        out_specs=P("orb", "pair", None),
        check_vma=False,
    )
```

```python
import functools

import jax
import jax.numpy as jnp
from jax import lax
from jax.experimental import pallas as pl
from jax.experimental.pallas import tpu as pltpu
from jax.sharding import PartitionSpec as P

LANES = 128
DEAD = -10000.0
f32, bf16 = jnp.float32, jnp.bfloat16


def repeat(start, stop, body):
    if stop - start <= 8:
        for k in range(start, stop):
            body(k)
    else:
        lax.fori_loop(start, stop, lambda k, c: (body(k), c)[1], 0)


def kernel(
    n_orb,
    n_pair,
    fold,
    orb_ref,
    send_ref,
    left_ref,
    off_ref,
    out_ref,
    slab,
    edges,
    raw,
    mine_a,
    boxes,
    sums,
    tab_pair,
    tab_orb,
    out_d,
    load_sem,
    send_a,
    recv_a,
    send_p,
    recv_p,
    send_i,
    recv_i,
    send_d,
    recv_d,
):
    owned, box_side, plane = orb_ref.shape
    slots = send_ref.shape[2]
    own_rows = box_side // n_pair
    side = owned * box_side
    me = lax.axis_index("orb")
    mine = lax.axis_index("pair")
    lines = n_orb // fold
    high, low = me // fold, lax.rem(me, fold)
    barrier = pltpu.get_barrier_semaphore()

    def other_orb(k):
        return lax.rem(me + k, n_orb)

    def other_pair(k):
        return lax.rem(mine + k, n_pair)

    def mate(k):
        return high * fold + lax.rem(low + k, fold)

    first = mine * fold
    below = jnp.maximum(first - 1, 0)
    above = jnp.minimum(first + fold, fold * n_pair - 1)

    def lanes_of(c, n):
        return pl.ds(pl.multiple_of(c * LANES, LANES), n * LANES)

    loads = [
        pltpu.make_async_copy(send_ref, raw.at[0], load_sem.at[0]),
        pltpu.make_async_copy(left_ref, raw.at[1], load_sem.at[1]),
        pltpu.make_async_copy(off_ref, raw.at[2], load_sem.at[2]),
        pltpu.make_async_copy(orb_ref.at[:, :, lanes_of(first, fold)], slab, load_sem.at[3]),
        pltpu.make_async_copy(orb_ref.at[:, :, lanes_of(below, 1)], edges.at[0], load_sem.at[4]),
        pltpu.make_async_copy(orb_ref.at[:, :, lanes_of(above, 1)], edges.at[1], load_sem.at[5]),
    ]
    for load in loads:
        load.start()

    def greet(o, q):
        pl.semaphore_signal(barrier, inc=1, device_id={"orb": o, "pair": q})

    repeat(1, n_orb, lambda k: greet(other_orb(k), mine))
    for j in range(fold):
        repeat(1, n_pair, lambda k: greet(mate(j), other_pair(k)))

    for load in loads[:3]:
        load.wait()
    sent, left, off = (raw[i, 0].astype(f32) for i in range(3))
    dead = left < 0
    tab_pair[mine, 0:1] = box_side * 2 * sent
    tab_pair[mine, 1:2] = jnp.where(dead, DEAD, box_side * 2 * left - off)
    tab_pair[mine, 2:3] = jnp.where(dead, DEAD, 2 * box_side * owned * left + off)
    tab_pair[mine, 3:4] = 2 * box_side * owned * sent

    for load in loads[3:]:
        load.wait()
    lane = lax.broadcasted_iota(jnp.int32, (box_side, LANES), 1)
    row = lax.broadcasted_iota(jnp.int32, (box_side, LANES), 0)
    for j in range(fold):
        halos = []
        for b in range(owned):
            value = slab[b, :, j * LANES : (j + 1) * LANES].astype(bf16)
            mine_a[j, b] = value
            lower = slab[b, :, (j - 1) * LANES : j * LANES] if j else edges[0, b]
            upper = slab[b, :, (j + 1) * LANES : (j + 2) * LANES] if j + 1 < fold else edges[1, b]
            ends_low = jnp.where(mine > 0, 0, LANES) if j == 0 else 0
            ends_high = jnp.where(mine < n_pair - 1, 0, LANES) if j + 1 == fold else 0
            has_below = lane + ends_low < box_side
            has_above = lane - ends_high >= LANES - box_side
            halo = jnp.where(has_below, pltpu.roll(lower, box_side, 1), 0.0)
            halo = jnp.where(has_above, pltpu.roll(upper, LANES - box_side, 1), halo)
            halos.append(halo if b == 0 else pltpu.roll(halo, b * 2 * box_side, 1))
        mine_a[j, owned] = functools.reduce(jnp.add, halos).astype(bf16)

    pl.semaphore_wait(barrier, n_orb - 1 + fold * (n_pair - 1))

    def copy_a(o, at):
        return pltpu.make_async_remote_copy(
            src_ref=mine_a.at[lax.rem(o, fold)],
            dst_ref=boxes.at[at],
            send_sem=send_a.at[o],
            recv_sem=recv_a.at[at],
            device_id={"orb": o},
        )

    def copy_p(q, at):
        return pltpu.make_async_remote_copy(
            src_ref=tab_pair.at[mine],
            dst_ref=tab_pair.at[at],
            send_sem=send_p.at[q],
            recv_sem=recv_p.at[at],
            device_id={"pair": q},
        )

    def copy_i(o, at):
        return pltpu.make_async_remote_copy(
            src_ref=tab_orb.at[me],
            dst_ref=tab_orb.at[at],
            send_sem=send_i.at[o],
            recv_sem=recv_i.at[at],
            device_id={"orb": o},
        )

    def block_of(o, q):
        return lax.rem(o, fold) + q * fold

    def copy_d(o, q, from_o, from_q):
        to, at = block_of(o, q), block_of(from_o, from_q)
        return pltpu.make_async_remote_copy(
            src_ref=out_d.at[to],
            dst_ref=out_ref.at[:, lanes_of(at, 1)],
            send_sem=send_d.at[to],
            recv_sem=recv_d.at[at],
            device_id={"orb": o, "pair": q},
        )

    repeat(1, n_pair, lambda k: copy_p(other_pair(k), mine).start())
    repeat(1, n_orb, lambda k: copy_a(other_orb(k), me).start())
    keep_a = pltpu.make_async_copy(mine_a.at[low], boxes.at[me], load_sem.at[0])
    keep_a.start()

    inner = lane % box_side < box_side - 1
    near = lane < LANES - box_side
    not_last = row < box_side - 1
    not_first = row > 0

    def up(v):
        return jnp.where(not_last, pltpu.roll(v, box_side - 1, 0), 0.0)

    def pieces(s, m):
        own = boxes[s, m].astype(f32)
        halo = boxes[s, owned].astype(f32)
        if m:
            halo = pltpu.roll(halo, LANES - m * 2 * box_side, 1)
        after = jnp.where(near, pltpu.roll(own, LANES - box_side, 1), halo)
        return own, after, halo

    def products(s):
        rows = []
        for m in range(owned):
            own, after, halo = pieces(s, m)
            beside = jnp.where(inner, pltpu.roll(own, LANES - 1, 1), 0.0)
            parts = [own * own, own * up(own), own * beside, own * after, own * halo]
            rows.append(jnp.concatenate([p.astype(bf16) for p in parts], axis=1))
        return jnp.concatenate(rows, axis=0)

    at_row = lax.broadcasted_iota(jnp.int32, (side, side), 0)
    at_col = lax.broadcasted_iota(jnp.int32, (side, side), 1)
    key = at_row % box_side - at_col % box_side
    key = key + 2 * box_side * (at_col // box_side) + 2 * box_side * owned * (at_row // box_side)
    key = key.astype(f32)
    slot = lax.broadcasted_iota(jnp.int32, (2 * n_pair, slots), 1)

    def counts(s):
        given = tab_orb[s, : 2 * n_pair].astype(f32)
        bands = []
        for j in range(fold):
            own_tab = tab_orb[high * fold + j, 2 * n_pair :].astype(f32)
            codes = jnp.where(slot == high * fold + j, given, 0.0) + jnp.where(slot == s, own_tab, 0.0)
            codes = jnp.sum(codes, axis=1, keepdims=True)
            total = jnp.zeros((side, side), f32)
            for u in range(2 * n_pair):
                total = total + jnp.where(key == codes[u : u + 1, :], 1.0, 0.0)
            bands.append(total.astype(bf16))
        return jnp.concatenate(bands, axis=0)

    def multiply(s):
        return jnp.dot(counts(s), products(s), preferred_element_type=f32)

    repeat(1, n_pair, lambda k: copy_p(other_pair(k), other_pair(k)).wait_recv())
    tab_orb[me] = jnp.concatenate(
        [tab_pair[p, r : r + 1] for r in range(4) for p in range(n_pair)], axis=0
    ).astype(bf16)
    repeat(1, n_orb, lambda k: copy_i(other_orb(k), me).start())
    for j in range(1, fold):
        copy_i(mate(j), mate(j)).wait_recv()
    keep_a.wait()
    sums[...] = multiply(me)
    for j in range(1, fold):
        copy_a(mate(j), mate(j)).wait_recv()
        sums[...] = sums[...] + multiply(mate(j))

    def process(k):
        for j in range(fold):
            s = lax.rem(high + k, lines) * fold + j
            copy_a(s, s).wait_recv()
            copy_i(s, s).wait_recv()
            sums[...] = sums[...] + multiply(s)

    repeat(1, lines, process)

    scale = -0.25 / 36.0
    for j in range(fold):
        fields = []
        for k in range(owned):
            own, after, halo = pieces(high * fold + j, k)

            def part(i):
                at = j * side + k * box_side
                return sums[at : at + box_side, i * LANES : (i + 1) * LANES]

            c_x, c_z, c_y = part(1), part(2), part(3)
            value = 6.0 * (part(0) * own) + c_x * up(own)
            value = value + jnp.where(not_first, pltpu.roll(c_x * own, 1, 0), 0.0)
            value = value + c_z * pltpu.roll(own, LANES - 1, 1) + pltpu.roll(c_z * own, 1, 1)
            value = value + c_y * after
            flux = pltpu.roll(c_y * own, box_side, 1)
            value = value + jnp.where(lane >= box_side, flux, part(4) * halo)
            fields.append(value * scale)
        for q in range(n_pair):
            at = slice(q * own_rows, (q + 1) * own_rows)
            rows = jnp.concatenate([v[at] for v in fields], axis=0)
            out_d[q * fold + j] = rows.astype(bf16)

    def each_other(body):
        for j in range(fold):
            repeat(0 if j else 1, n_pair, lambda k: body(mate(j), other_pair(k)))

    each_other(lambda o, q: copy_d(o, q, me, mine).start())
    keep = pltpu.make_async_copy(
        out_d.at[block_of(me, mine)],
        out_ref.at[:, lanes_of(block_of(me, mine), 1)],
        load_sem.at[0],
    )
    keep.start()
    repeat(1, n_orb, lambda k: copy_a(other_orb(k), me).wait_send())
    repeat(1, n_orb, lambda k: copy_i(other_orb(k), me).wait_send())
    repeat(1, n_pair, lambda k: copy_p(other_pair(k), mine).wait_send())
    keep.wait()
    each_other(lambda o, q: copy_d(o, q, o, q).wait_recv())
    each_other(lambda o, q: copy_d(o, q, me, mine).wait_send())


def local(n_orb, n_pair, orbitals, send_index, pair_left, pair_offset):
    owned, box_side, plane = orbitals.shape
    slots = send_index.shape[2]
    own_rows = box_side // n_pair
    fold = plane // n_pair // LANES
    assert owned * 2 * box_side == LANES and slots == n_orb
    assert n_orb % fold == 0 and plane == fold * n_pair * LANES
    inputs = (orbitals, send_index, pair_left, pair_offset)
    hbm = pl.BlockSpec(memory_space=pltpu.HBM)
    anywhere = pl.BlockSpec(memory_space=pl.ANY)
    dma = pltpu.SemaphoreType.DMA
    field = pl.pallas_call(
        functools.partial(kernel, n_orb, n_pair, fold),
        out_shape=jax.ShapeDtypeStruct((owned * own_rows, plane), bf16),
        in_specs=[hbm] * 4,
        out_specs=anywhere,
        scratch_shapes=[
            pltpu.VMEM((owned, box_side, fold * LANES), f32),
            pltpu.VMEM((2, owned, box_side, LANES), f32),
            pltpu.VMEM((3, 1, 1, slots), jnp.int32),
            pltpu.VMEM((fold, owned + 1, box_side, LANES), bf16),
            pltpu.VMEM((n_orb, owned + 1, box_side, LANES), bf16),
            pltpu.VMEM((fold * owned * box_side, 5 * LANES), f32),
            pltpu.VMEM((n_pair, 4, slots), f32),
            pltpu.VMEM((n_orb, 4 * n_pair, slots), bf16),
            pltpu.VMEM((n_pair * fold, owned * own_rows, LANES), bf16),
            dma((6,)),
            dma((n_orb,)),
            dma((n_orb,)),
            dma((n_pair,)),
            dma((n_pair,)),
            dma((n_orb,)),
            dma((n_orb,)),
            dma((n_pair * fold,)),
            dma((n_pair * fold,)),
        ],
        compiler_params=pltpu.CompilerParams(
            collective_id=0, has_side_effects=True, vmem_limit_bytes=16 << 20
        ),
        name="exchange",
    )(*(pltpu.with_memory_space_constraint(x, pltpu.HBM) for x in inputs))
    return field.astype(f32).reshape(owned, own_rows, plane)


def solution(mesh):
    n_orb, n_pair = mesh.shape["orb"], mesh.shape["pair"]
    return jax.shard_map(
        functools.partial(local, n_orb, n_pair),
        mesh=mesh,
        in_specs=(
            P("orb", None, None),
            P("orb", "pair", None),
            P("orb", "pair", None),
            P("orb", "pair", None),
        ),
        out_specs=P("orb", "pair", None),
        check_vma=False,
    )
```

```python
import functools

import jax
import jax.numpy as jnp
from jax import lax
from jax.experimental import pallas as pl
from jax.experimental.pallas import tpu as pltpu
from jax.sharding import PartitionSpec as P

LANES = 128
DEAD = -10000.0
f32, bf16 = jnp.float32, jnp.bfloat16


def repeat(start, stop, body):
    if stop - start <= 8:
        for k in range(start, stop):
            body(k)
    else:
        lax.fori_loop(start, stop, lambda k, c: (body(k), c)[1], 0)


def kernel(
    n_orb,
    n_pair,
    fold,
    orb_ref,
    send_ref,
    left_ref,
    off_ref,
    out_ref,
    slab,
    edges,
    raw,
    mine_a,
    boxes,
    sums,
    halves,
    tables,
    out_d,
    load_sem,
    send_a,
    recv_a,
    send_p,
    recv_p,
    send_i,
    recv_i,
    send_d,
    recv_d,
):
    owned, box_side, plane = orb_ref.shape
    slots = send_ref.shape[2]
    own_rows = box_side // n_pair
    side = owned * box_side
    me = lax.axis_index("orb")
    mine = lax.axis_index("pair")
    lines = n_orb // fold
    high, low = me // fold, lax.rem(me, fold)
    barrier = pltpu.get_barrier_semaphore()

    def other_orb(k):
        return lax.rem(me + k, n_orb)

    def other_pair(k):
        return lax.rem(mine + k, n_pair)

    twin = 2 if n_pair % 2 == 0 else 1
    chips = n_pair // twin
    chip, core = mine // twin, lax.rem(mine, twin)
    entries = 4 * twin
    pack = LANES // slots

    def other_core(k):
        return chip * twin + lax.rem(core + k, twin)

    def same_core(c):
        return lax.rem(chip + c, chips) * twin + core

    def each_table(body):
        for c in range(chips):
            repeat(0 if c else 1, n_orb, lambda k: body(other_orb(k), same_core(c)))

    def mate(k):
        return high * fold + lax.rem(low + k, fold)

    first = mine * fold
    below = jnp.maximum(first - 1, 0)
    above = jnp.minimum(first + fold, fold * n_pair - 1)

    def lanes_of(c, n):
        return pl.ds(pl.multiple_of(c * LANES, LANES), n * LANES)

    loads = [
        pltpu.make_async_copy(send_ref, raw.at[0], load_sem.at[0]),
        pltpu.make_async_copy(left_ref, raw.at[1], load_sem.at[0]),
        pltpu.make_async_copy(off_ref, raw.at[2], load_sem.at[0]),
        pltpu.make_async_copy(orb_ref.at[:, :, lanes_of(first, fold)], slab, load_sem.at[1]),
        pltpu.make_async_copy(orb_ref.at[:, :, lanes_of(below, 1)], edges.at[0], load_sem.at[2]),
        pltpu.make_async_copy(orb_ref.at[:, :, lanes_of(above, 1)], edges.at[1], load_sem.at[2]),
    ]
    for load in loads:
        load.start()

    def greet(o, q):
        pl.semaphore_signal(barrier, inc=1, device_id={"orb": o, "pair": q})

    each_table(greet)
    for j in range(fold):
        for c in range(chips):
            for k in range(1, twin):
                greet(mate(j), lax.rem(chip + c, chips) * twin + lax.rem(core + k, twin))

    pltpu.make_async_copy(raw, raw, load_sem.at[0]).wait()
    wide = lax.broadcasted_iota(jnp.int32, (1, LANES), 1)
    sent, left, off = (
        jnp.concatenate([raw[i, 0].astype(f32), jnp.zeros((1, LANES - slots), f32)], axis=1)
        if slots < LANES
        else raw[i, 0].astype(f32)
        for i in range(3)
    )
    dead = left < 0
    table = [
        box_side * 2 * sent,
        jnp.where(dead, DEAD, box_side * 2 * left - off),
        jnp.where(dead, DEAD, 2 * box_side * owned * left + off),
        2 * box_side * owned * sent,
    ]
    for i in range(halves.shape[1]):
        line = jnp.zeros((1, LANES), f32)
        for e in range(i * pack, min((i + 1) * pack, entries)):
            at = (e % pack) * slots
            value = pltpu.roll(table[e % 4], at, 1) if at else table[e % 4]
            line = line + jnp.where(core == e // 4, value, 0.0)
        halves[0, i : i + 1] = line

    loads[3].wait()
    pltpu.make_async_copy(edges, edges, load_sem.at[2]).wait()
    lane = lax.broadcasted_iota(jnp.int32, (box_side, LANES), 1)
    row = lax.broadcasted_iota(jnp.int32, (box_side, LANES), 0)
    for j in range(fold):
        halos = []
        for b in range(owned):
            value = slab[b, :, j * LANES : (j + 1) * LANES].astype(bf16)
            mine_a[j, b] = value
            lower = slab[b, :, (j - 1) * LANES : j * LANES] if j else edges[0, b]
            upper = slab[b, :, (j + 1) * LANES : (j + 2) * LANES] if j + 1 < fold else edges[1, b]
            ends_low = jnp.where(mine > 0, 0, LANES) if j == 0 else 0
            ends_high = jnp.where(mine < n_pair - 1, 0, LANES) if j + 1 == fold else 0
            has_below = lane + ends_low < box_side
            has_above = lane - ends_high >= LANES - box_side
            halo = jnp.where(has_below, pltpu.roll(lower, box_side, 1), 0.0)
            halo = jnp.where(has_above, pltpu.roll(upper, LANES - box_side, 1), halo)
            halos.append(halo if b == 0 else pltpu.roll(halo, b * 2 * box_side, 1))
        mine_a[j, owned] = functools.reduce(jnp.add, halos).astype(bf16)

    pl.semaphore_wait(barrier, n_orb * chips - 1 + fold * chips * (twin - 1))

    def copy_a(o, at):
        return pltpu.make_async_remote_copy(
            src_ref=mine_a.at[lax.rem(o, fold)],
            dst_ref=boxes.at[at],
            send_sem=send_a,
            recv_sem=recv_a.at[at],
            device_id={"orb": o},
        )

    def copy_p(k):
        return pltpu.make_async_remote_copy(
            src_ref=halves.at[0],
            dst_ref=halves.at[k],
            send_sem=send_p.at[k],
            recv_sem=recv_p.at[k],
            device_id={"pair": other_core(k)},
        )

    def copy_i(o, q, from_o, from_q):
        return pltpu.make_async_remote_copy(
            src_ref=tables.at[me * chips + chip],
            dst_ref=tables.at[from_o * chips + from_q // twin],
            send_sem=send_i,
            recv_sem=recv_i,
            device_id={"orb": o, "pair": q},
        )

    def all_of(part, send_sem, recv_sem):
        return pltpu.make_async_remote_copy(
            src_ref=part,
            dst_ref=part,
            send_sem=send_sem,
            recv_sem=recv_sem,
            device_id={"orb": other_orb(1)},
        )

    def block_of(o, q):
        return lax.rem(o, fold) + q * fold

    def copy_d(o, q, from_o, from_q):
        to, at = block_of(o, q), block_of(from_o, from_q)
        return pltpu.make_async_remote_copy(
            src_ref=out_d.at[to],
            dst_ref=out_ref.at[:, lanes_of(at, 1)],
            send_sem=send_d,
            recv_sem=recv_d,
            device_id={"orb": o, "pair": q},
        )

    for k in range(1, twin):
        copy_p(k).start()
    keep_a = pltpu.make_async_copy(mine_a.at[low], boxes.at[me], load_sem.at[0])
    keep_a.start()

    inner = lane % box_side < box_side - 1
    near = lane < LANES - box_side
    not_last = row < box_side - 1
    not_first = row > 0

    def up(v):
        return jnp.where(not_last, pltpu.roll(v, box_side - 1, 0), 0.0)

    def pieces(s, m):
        own = boxes[s, m].astype(f32)
        halo = boxes[s, owned].astype(f32)
        if m:
            halo = pltpu.roll(halo, LANES - m * 2 * box_side, 1)
        after = jnp.where(near, pltpu.roll(own, LANES - box_side, 1), halo)
        return own, after, halo

    def products(s):
        rows = []
        for m in range(owned):
            own, after, halo = pieces(s, m)
            beside = jnp.where(inner, pltpu.roll(own, LANES - 1, 1), 0.0)
            parts = [own * own, own * up(own), own * beside, own * after, own * halo]
            rows.append(jnp.concatenate([p.astype(bf16) for p in parts], axis=1))
        return jnp.concatenate(rows, axis=0)

    at_row = lax.broadcasted_iota(jnp.int32, (side, side), 0)
    at_col = lax.broadcasted_iota(jnp.int32, (side, side), 1)
    key = at_row % box_side - at_col % box_side
    key = key + 2 * box_side * (at_col // box_side) + 2 * box_side * owned * (at_row // box_side)
    key = key.astype(f32)
    use = lax.broadcasted_iota(jnp.int32, (2 * n_pair, LANES), 0)
    use_lane = lax.broadcasted_iota(jnp.int32, (2 * n_pair, LANES), 1)
    use_chip = use % n_pair // twin
    use_given = use % twin * 4 + use // n_pair
    use_own = use_given + 2

    def rows_of(o, entry):
        found = jnp.zeros((2 * n_pair, LANES), f32)
        for c in range(chips):
            for i in range(halves.shape[1]):
                here = (use_chip == c) & (entry // pack == i)
                found = jnp.where(here, tables[o * chips + c, i : i + 1], found)
        return found

    def counts(s, own_tabs):
        given = rows_of(s, use_given)
        bands = []
        for j in range(fold):
            codes = jnp.where(use_lane == use_given % pack * slots + high * fold + j, given, 0.0)
            codes = codes + jnp.where(use_lane == use_own % pack * slots + s, own_tabs[j], 0.0)
            codes = jnp.sum(codes, axis=1, keepdims=True)
            total = jnp.zeros((side, side), f32)
            for u in range(2 * n_pair):
                total = total + jnp.where(key == codes[u : u + 1, :], 1.0, 0.0)
            bands.append(total.astype(bf16))
        return jnp.concatenate(bands, axis=0)

    for k in range(1, twin):
        copy_p(k).wait_recv()
    tables[me * chips + chip] = functools.reduce(jnp.add, [halves[k] for k in range(twin)])
    each_table(lambda o, q: copy_i(o, q, me, mine).start())
    repeat(1, n_orb, lambda k: copy_a(other_orb(k), me).start())

    all_tables = all_of(tables.at[pl.ds(0, n_orb * chips - 1)], send_i, recv_i)
    all_tables.wait_recv()
    own_tabs = [rows_of(high * fold + j, use_own) for j in range(fold)]

    def multiply(s):
        return jnp.dot(counts(s, own_tabs), products(s), preferred_element_type=f32)

    keep_a.wait()
    sums[...] = multiply(me)
    for j in range(1, fold):
        copy_a(mate(j), mate(j)).wait_recv()
        sums[...] = sums[...] + multiply(mate(j))

    def process(k):
        for j in range(fold):
            s = lax.rem(high + k, lines) * fold + j
            copy_a(s, s).wait_recv()
            sums[...] = sums[...] + multiply(s)

    repeat(1, lines, process)

    scale = -0.25 / 36.0
    for j in range(fold):
        fields = []
        for k in range(owned):
            own, after, halo = pieces(high * fold + j, k)

            def part(i):
                at = j * side + k * box_side
                return sums[at : at + box_side, i * LANES : (i + 1) * LANES]

            c_x, c_z, c_y = part(1), part(2), part(3)
            value = 6.0 * (part(0) * own) + c_x * up(own)
            value = value + jnp.where(not_first, pltpu.roll(c_x * own, 1, 0), 0.0)
            value = value + c_z * pltpu.roll(own, LANES - 1, 1) + pltpu.roll(c_z * own, 1, 1)
            value = value + c_y * after
            flux = pltpu.roll(c_y * own, box_side, 1)
            value = value + jnp.where(lane >= box_side, flux, part(4) * halo)
            fields.append(value * scale)
        for q in range(n_pair):
            at = slice(q * own_rows, (q + 1) * own_rows)
            rows = jnp.concatenate([v[at] for v in fields], axis=0)
            out_d[q * fold + j] = rows.astype(bf16)

    def each_other(body):
        for j in range(fold):
            repeat(0 if j else 1, n_pair, lambda k: body(mate(j), other_pair(k)))

    each_other(lambda o, q: copy_d(o, q, me, mine).start())
    keep = pltpu.make_async_copy(
        out_d.at[block_of(me, mine)],
        out_ref.at[:, lanes_of(block_of(me, mine), 1)],
        load_sem.at[0],
    )
    keep.start()
    all_of(boxes.at[pl.ds(0, n_orb - 1)], send_a, send_a).wait_send()
    all_tables.wait_send()
    for k in range(1, twin):
        copy_p(k).wait_send()
    keep.wait()
    all_fields = all_of(out_ref.at[:, lanes_of(0, n_pair * fold - 1)], send_d, recv_d)
    all_fields.wait_recv()
    all_fields.wait_send()


def local(n_orb, n_pair, orbitals, send_index, pair_left, pair_offset):
    owned, box_side, plane = orbitals.shape
    slots = send_index.shape[2]
    own_rows = box_side // n_pair
    fold = plane // n_pair // LANES
    assert owned * 2 * box_side == LANES and slots == n_orb
    assert n_orb % fold == 0 and plane == fold * n_pair * LANES
    twin = 2 if n_pair % 2 == 0 else 1
    lines = -(-4 * twin // (LANES // slots))
    inputs = (orbitals, send_index, pair_left, pair_offset)
    hbm = pl.BlockSpec(memory_space=pltpu.HBM)
    anywhere = pl.BlockSpec(memory_space=pl.ANY)
    dma = pltpu.SemaphoreType.DMA
    field = pl.pallas_call(
        functools.partial(kernel, n_orb, n_pair, fold),
        out_shape=jax.ShapeDtypeStruct((owned * own_rows, plane), bf16),
        in_specs=[hbm] * 4,
        out_specs=anywhere,
        scratch_shapes=[
            pltpu.VMEM((owned, box_side, fold * LANES), f32),
            pltpu.VMEM((2, owned, box_side, LANES), f32),
            pltpu.VMEM((3, 1, 1, slots), jnp.int32),
            pltpu.VMEM((fold, owned + 1, box_side, LANES), bf16),
            pltpu.VMEM((n_orb, owned + 1, box_side, LANES), bf16),
            pltpu.VMEM((fold * owned * box_side, 5 * LANES), f32),
            pltpu.VMEM((twin, lines, LANES), f32),
            pltpu.VMEM((n_orb * n_pair // twin, lines, LANES), f32),
            pltpu.VMEM((n_pair * fold, owned * own_rows, LANES), bf16),
            dma((3,)),
            dma,
            dma((n_orb,)),
            dma((twin,)),
            dma((twin,)),
            dma,
            dma,
            dma,
            dma,
        ],
        compiler_params=pltpu.CompilerParams(
            collective_id=0, has_side_effects=True, vmem_limit_bytes=16 << 20
        ),
        name="exchange",
    )(*(pltpu.with_memory_space_constraint(x, pltpu.HBM) for x in inputs))
    return field.astype(f32).reshape(owned, own_rows, plane)


def solution(mesh):
    n_orb, n_pair = mesh.shape["orb"], mesh.shape["pair"]
    return jax.shard_map(
        functools.partial(local, n_orb, n_pair),
        mesh=mesh,
        in_specs=(
            P("orb", None, None),
            P("orb", "pair", None),
            P("orb", "pair", None),
            P("orb", "pair", None),
        ),
        out_specs=P("orb", "pair", None),
        check_vma=False,
    )
```

```python
import functools

import jax
import jax.numpy as jnp
from jax import lax
from jax.experimental import pallas as pl
from jax.experimental.pallas import tpu as pltpu
from jax.sharding import PartitionSpec as P

LANES = 128
DEAD = -10000.0
f32, bf16 = jnp.float32, jnp.bfloat16


def repeat(start, stop, body):
    if stop - start <= 8:
        for k in range(start, stop):
            body(k)
    else:
        lax.fori_loop(start, stop, lambda k, c: (body(k), c)[1], 0)


def kernel(
    n_orb,
    n_pair,
    fold,
    orb_ref,
    send_ref,
    left_ref,
    off_ref,
    out_ref,
    slab,
    edges,
    raw,
    mine_a,
    boxes,
    sums,
    halves,
    tables,
    out_d,
    load_sem,
    send_a,
    recv_a,
    send_p,
    recv_p,
    send_i,
    recv_i,
    send_d,
    recv_d,
):
    owned, box_side, plane = orb_ref.shape
    slots = send_ref.shape[2]
    own_rows = box_side // n_pair
    side = owned * box_side
    me = lax.axis_index("orb")
    mine = lax.axis_index("pair")
    lines = n_orb // fold
    high, low = me // fold, lax.rem(me, fold)
    barrier = pltpu.get_barrier_semaphore()

    def other_orb(k):
        return lax.rem(me + k, n_orb)

    def other_pair(k):
        return lax.rem(mine + k, n_pair)

    twin = 2 if n_pair % 2 == 0 else 1
    chips = n_pair // twin
    chip, core = mine // twin, lax.rem(mine, twin)
    entries = 4 * twin
    pack = LANES // slots

    def other_core(k):
        return chip * twin + lax.rem(core + k, twin)

    def same_core(c):
        return lax.rem(chip + c, chips) * twin + core

    def each_table(body):
        for c in range(chips):
            repeat(0 if c else 1, n_orb, lambda k: body(other_orb(k), same_core(c)))

    half = lines // 2 if lines % 2 == 0 else lines
    span = lines // half

    def stripe(k):
        return lax.rem(high // half + k // half, span) * half + lax.rem(high + lax.rem(k, half), half)

    def mate(k):
        return high * fold + lax.rem(low + k, fold)

    first = mine * fold
    below = jnp.maximum(first - 1, 0)
    above = jnp.minimum(first + fold, fold * n_pair - 1)

    def lanes_of(c, n):
        return pl.ds(pl.multiple_of(c * LANES, LANES), n * LANES)

    def greet(o, q):
        pl.semaphore_signal(barrier, inc=1, device_id={"orb": o, "pair": q})

    each_table(greet)
    for j in range(fold):
        for c in range(chips):
            for k in range(1, twin):
                greet(mate(j), lax.rem(chip + c, chips) * twin + lax.rem(core + k, twin))

    loads = [
        pltpu.make_async_copy(send_ref, raw.at[0], load_sem.at[0]),
        pltpu.make_async_copy(left_ref, raw.at[1], load_sem.at[0]),
        pltpu.make_async_copy(off_ref, raw.at[2], load_sem.at[0]),
        pltpu.make_async_copy(orb_ref.at[:, :, lanes_of(first, fold)], slab, load_sem.at[1]),
        pltpu.make_async_copy(orb_ref.at[:, :, lanes_of(below, 1)], edges.at[0], load_sem.at[2]),
        pltpu.make_async_copy(orb_ref.at[:, :, lanes_of(above, 1)], edges.at[1], load_sem.at[2]),
    ]
    for load in loads:
        load.start()

    pltpu.make_async_copy(raw, raw, load_sem.at[0]).wait()
    wide = lax.broadcasted_iota(jnp.int32, (1, LANES), 1)
    sent, left, off = (
        jnp.concatenate([raw[i, 0].astype(f32), jnp.zeros((1, LANES - slots), f32)], axis=1)
        if slots < LANES
        else raw[i, 0].astype(f32)
        for i in range(3)
    )
    dead = left < 0
    table = [
        box_side * 2 * sent,
        jnp.where(dead, DEAD, box_side * 2 * left - off),
        jnp.where(dead, DEAD, 2 * box_side * owned * left + off),
        2 * box_side * owned * sent,
    ]
    for i in range(halves.shape[1]):
        line = jnp.zeros((1, LANES), f32)
        for e in range(i * pack, min((i + 1) * pack, entries)):
            at = (e % pack) * slots
            value = pltpu.roll(table[e % 4], at, 1) if at else table[e % 4]
            line = line + jnp.where(core == e // 4, value, 0.0)
        halves[0, i : i + 1] = line

    loads[3].wait()
    pltpu.make_async_copy(edges, edges, load_sem.at[2]).wait()
    lane = lax.broadcasted_iota(jnp.int32, (box_side, LANES), 1)
    row = lax.broadcasted_iota(jnp.int32, (box_side, LANES), 0)
    for j in range(fold):
        halos = []
        for b in range(owned):
            value = slab[b, :, j * LANES : (j + 1) * LANES].astype(bf16)
            mine_a[j, b] = value
            lower = slab[b, :, (j - 1) * LANES : j * LANES] if j else edges[0, b]
            upper = slab[b, :, (j + 1) * LANES : (j + 2) * LANES] if j + 1 < fold else edges[1, b]
            ends_low = jnp.where(mine > 0, 0, LANES) if j == 0 else 0
            ends_high = jnp.where(mine < n_pair - 1, 0, LANES) if j + 1 == fold else 0
            has_below = lane + ends_low < box_side
            has_above = lane - ends_high >= LANES - box_side
            halo = jnp.where(has_below, pltpu.roll(lower, box_side, 1), 0.0)
            halo = jnp.where(has_above, pltpu.roll(upper, LANES - box_side, 1), halo)
            halos.append(halo if b == 0 else pltpu.roll(halo, b * 2 * box_side, 1))
        mine_a[j, owned] = functools.reduce(jnp.add, halos).astype(bf16)

    pl.semaphore_wait(barrier, n_orb * chips - 1 + fold * chips * (twin - 1))

    def copy_a(o, at):
        return pltpu.make_async_remote_copy(
            src_ref=mine_a.at[lax.rem(o, fold)],
            dst_ref=boxes.at[at],
            send_sem=send_a,
            recv_sem=recv_a.at[at],
            device_id={"orb": o},
        )

    def copy_p(k):
        return pltpu.make_async_remote_copy(
            src_ref=halves.at[0],
            dst_ref=halves.at[k],
            send_sem=send_p.at[k],
            recv_sem=recv_p.at[k],
            device_id={"pair": other_core(k)},
        )

    def copy_i(o, q, from_o, from_q):
        return pltpu.make_async_remote_copy(
            src_ref=tables.at[me * chips + chip],
            dst_ref=tables.at[from_o * chips + from_q // twin],
            send_sem=send_i,
            recv_sem=recv_i,
            device_id={"orb": o, "pair": q},
        )

    def all_of(part, send_sem, recv_sem):
        return pltpu.make_async_remote_copy(
            src_ref=part,
            dst_ref=part,
            send_sem=send_sem,
            recv_sem=recv_sem,
            device_id={"orb": other_orb(1)},
        )

    def block_of(o, q):
        return lax.rem(o, fold) + q * fold

    def copy_d(o, q, from_o, from_q):
        to, at = block_of(o, q), block_of(from_o, from_q)
        return pltpu.make_async_remote_copy(
            src_ref=out_d.at[to],
            dst_ref=out_ref.at[:, lanes_of(at, 1)],
            send_sem=send_d,
            recv_sem=recv_d,
            device_id={"orb": o, "pair": q},
        )

    for k in range(1, twin):
        copy_p(k).start()
    keep_a = pltpu.make_async_copy(mine_a.at[low], boxes.at[me], load_sem.at[0])
    keep_a.start()

    inner = lane % box_side < box_side - 1
    near = lane < LANES - box_side
    not_last = row < box_side - 1
    not_first = row > 0

    def up(v):
        return jnp.where(not_last, pltpu.roll(v, box_side - 1, 0), 0.0)

    def pieces(s, m):
        own = boxes[s, m].astype(f32)
        halo = boxes[s, owned].astype(f32)
        if m:
            halo = pltpu.roll(halo, LANES - m * 2 * box_side, 1)
        after = jnp.where(near, pltpu.roll(own, LANES - box_side, 1), halo)
        return own, after, halo

    def products(s):
        rows = []
        for m in range(owned):
            own, after, halo = pieces(s, m)
            beside = jnp.where(inner, pltpu.roll(own, LANES - 1, 1), 0.0)
            parts = [own * own, own * up(own), own * beside, own * after, own * halo]
            rows.append(jnp.concatenate([p.astype(bf16) for p in parts], axis=1))
        return jnp.concatenate(rows, axis=0)

    at_row = lax.broadcasted_iota(jnp.int32, (side, side), 0)
    at_col = lax.broadcasted_iota(jnp.int32, (side, side), 1)
    key = at_row % box_side - at_col % box_side
    key = key + 2 * box_side * (at_col // box_side) + 2 * box_side * owned * (at_row // box_side)
    key = key.astype(f32)
    use = lax.broadcasted_iota(jnp.int32, (2 * n_pair, LANES), 0)
    use_lane = lax.broadcasted_iota(jnp.int32, (2 * n_pair, LANES), 1)
    use_chip = use % n_pair // twin
    use_given = use % twin * 4 + use // n_pair
    use_own = use_given + 2

    def rows_of(o, entry):
        found = jnp.zeros((2 * n_pair, LANES), f32)
        for c in range(chips):
            for i in range(halves.shape[1]):
                here = (use_chip == c) & (entry // pack == i)
                found = jnp.where(here, tables[o * chips + c, i : i + 1], found)
        return found

    def counts(s, own_tabs):
        given = rows_of(s, use_given)
        bands = []
        for j in range(fold):
            codes = jnp.where(use_lane == use_given % pack * slots + high * fold + j, given, 0.0)
            codes = codes + jnp.where(use_lane == use_own % pack * slots + s, own_tabs[j], 0.0)
            codes = jnp.sum(codes, axis=1, keepdims=True)
            total = jnp.zeros((side, side), f32)
            for u in range(2 * n_pair):
                total = total + jnp.where(key == codes[u : u + 1, :], 1.0, 0.0)
            bands.append(total.astype(bf16))
        return jnp.concatenate(bands, axis=0)

    for k in range(1, twin):
        copy_p(k).wait_recv()
    tables[me * chips + chip] = functools.reduce(jnp.add, [halves[k] for k in range(twin)])
    each_table(lambda o, q: copy_i(o, q, me, mine).start())
    def send_line(k):
        for j in range(fold):
            copy_a(stripe(k) * fold + lax.rem(low + j, fold), me).start()

    repeat(half, lines, send_line)
    repeat(1, half, send_line)
    for j in range(1, fold):
        copy_a(mate(j), me).start()

    all_tables = all_of(tables.at[pl.ds(0, n_orb * chips - 1)], send_i, recv_i)
    all_tables.wait_recv()
    own_tabs = [rows_of(high * fold + j, use_own) for j in range(fold)]

    def multiply(s):
        return jnp.dot(counts(s, own_tabs), products(s), preferred_element_type=f32)

    keep_a.wait()
    sums[...] = multiply(me)
    for j in range(1, fold):
        copy_a(mate(j), mate(j)).wait_recv()
        sums[...] = sums[...] + multiply(mate(j))

    def process(k):
        for j in range(fold):
            s = stripe(k) * fold + lax.rem(low + j, fold)
            copy_a(s, s).wait_recv()
            sums[...] = sums[...] + multiply(s)

    repeat(1, lines, process)

    scale = -0.25 / 36.0
    for j in range(fold):
        fields = []
        for k in range(owned):
            own, after, halo = pieces(high * fold + j, k)

            def part(i):
                at = j * side + k * box_side
                return sums[at : at + box_side, i * LANES : (i + 1) * LANES]

            c_x, c_z, c_y = part(1), part(2), part(3)
            value = 6.0 * (part(0) * own) + c_x * up(own)
            value = value + jnp.where(not_first, pltpu.roll(c_x * own, 1, 0), 0.0)
            value = value + c_z * pltpu.roll(own, LANES - 1, 1) + pltpu.roll(c_z * own, 1, 1)
            value = value + c_y * after
            flux = pltpu.roll(c_y * own, box_side, 1)
            value = value + jnp.where(lane >= box_side, flux, part(4) * halo)
            fields.append(value * scale)
        for q in range(n_pair):
            at = slice(q * own_rows, (q + 1) * own_rows)
            rows = jnp.concatenate([v[at] for v in fields], axis=0)
            out_d[q * fold + j] = rows.astype(bf16)

    def each_other(body):
        for j in reversed(range(fold)):
            repeat(0 if j else 1, n_pair, lambda k: body(mate(j), other_pair(k)))

    each_other(lambda o, q: copy_d(o, q, me, mine).start())
    keep = pltpu.make_async_copy(
        out_d.at[block_of(me, mine)],
        out_ref.at[:, lanes_of(block_of(me, mine), 1)],
        load_sem.at[0],
    )
    keep.start()
    all_of(boxes.at[pl.ds(0, n_orb - 1)], send_a, send_a).wait_send()
    all_tables.wait_send()
    for k in range(1, twin):
        copy_p(k).wait_send()
    keep.wait()
    all_fields = all_of(out_ref.at[:, lanes_of(0, n_pair * fold - 1)], send_d, recv_d)
    all_fields.wait_recv()
    all_fields.wait_send()


def local(n_orb, n_pair, orbitals, send_index, pair_left, pair_offset):
    owned, box_side, plane = orbitals.shape
    slots = send_index.shape[2]
    own_rows = box_side // n_pair
    fold = plane // n_pair // LANES
    assert owned * 2 * box_side == LANES and slots == n_orb
    assert n_orb % fold == 0 and plane == fold * n_pair * LANES
    twin = 2 if n_pair % 2 == 0 else 1
    lines = -(-4 * twin // (LANES // slots))
    inputs = (orbitals, send_index, pair_left, pair_offset)
    hbm = pl.BlockSpec(memory_space=pltpu.HBM)
    anywhere = pl.BlockSpec(memory_space=pl.ANY)
    dma = pltpu.SemaphoreType.DMA
    field = pl.pallas_call(
        functools.partial(kernel, n_orb, n_pair, fold),
        out_shape=jax.ShapeDtypeStruct((owned * own_rows, plane), bf16),
        in_specs=[hbm] * 4,
        out_specs=anywhere,
        scratch_shapes=[
            pltpu.VMEM((owned, box_side, fold * LANES), f32),
            pltpu.VMEM((2, owned, box_side, LANES), f32),
            pltpu.VMEM((3, 1, 1, slots), jnp.int32),
            pltpu.VMEM((fold, owned + 1, box_side, LANES), bf16),
            pltpu.VMEM((n_orb, owned + 1, box_side, LANES), bf16),
            pltpu.VMEM((fold * owned * box_side, 5 * LANES), f32),
            pltpu.VMEM((twin, lines, LANES), f32),
            pltpu.VMEM((n_orb * n_pair // twin, lines, LANES), f32),
            pltpu.VMEM((n_pair * fold, owned * own_rows, LANES), bf16),
            dma((3,)),
            dma,
            dma((n_orb,)),
            dma((twin,)),
            dma((twin,)),
            dma,
            dma,
            dma,
            dma,
        ],
        compiler_params=pltpu.CompilerParams(
            collective_id=0, has_side_effects=True, vmem_limit_bytes=16 << 20
        ),
        name="exchange",
    )(*(pltpu.with_memory_space_constraint(x, pltpu.HBM) for x in inputs))
    return field.astype(f32).reshape(owned, own_rows, plane)


def solution(mesh):
    n_orb, n_pair = mesh.shape["orb"], mesh.shape["pair"]
    return jax.shard_map(
        functools.partial(local, n_orb, n_pair),
        mesh=mesh,
        in_specs=(
            P("orb", None, None),
            P("orb", "pair", None),
            P("orb", "pair", None),
            P("orb", "pair", None),
        ),
        out_specs=P("orb", "pair", None),
        check_vma=False,
    )
```

```python
import functools

import jax
import jax.numpy as jnp
from jax import lax
from jax.experimental import pallas as pl
from jax.experimental.pallas import tpu as pltpu
from jax.sharding import PartitionSpec as P

LANES = 128
DEAD = -10000.0
f32, bf16 = jnp.float32, jnp.bfloat16


def repeat(start, stop, body):
    if stop - start <= 8:
        for k in range(start, stop):
            body(k)
    else:
        lax.fori_loop(start, stop, lambda k, c: (body(k), c)[1], 0)


def kernel(
    n_orb,
    n_pair,
    fold,
    orb_ref,
    send_ref,
    left_ref,
    off_ref,
    out_ref,
    slab,
    edges,
    raw,
    mine_a,
    boxes,
    sums,
    halves,
    tables,
    bands,
    out_d,
    load_sem,
    send_a,
    recv_a,
    send_p,
    recv_p,
    send_i,
    recv_i,
    send_d,
    recv_d,
):
    owned, box_side, plane = orb_ref.shape
    slots = send_ref.shape[2]
    own_rows = box_side // n_pair
    side = owned * box_side
    me = lax.axis_index("orb")
    mine = lax.axis_index("pair")
    lines = n_orb // fold
    high, low = me // fold, lax.rem(me, fold)
    barrier = pltpu.get_barrier_semaphore()

    def other_orb(k):
        return lax.rem(me + k, n_orb)

    def other_pair(k):
        return lax.rem(mine + k, n_pair)

    twin = 2 if n_pair % 2 == 0 else 1
    chips = n_pair // twin
    chip, core = mine // twin, lax.rem(mine, twin)
    entries = 4 * twin
    pack = LANES // slots

    def other_core(k):
        return chip * twin + lax.rem(core + k, twin)

    def same_core(c):
        return lax.rem(chip + c, chips) * twin + core

    def each_table(body):
        for c in range(chips):
            repeat(0 if c else 1, n_orb, lambda k: body(other_orb(k), same_core(c)))

    half = lines // 2 if lines % 2 == 0 else lines
    span = lines // half

    def stripe(k):
        return lax.rem(high // half + k // half, span) * half + lax.rem(high + lax.rem(k, half), half)

    def mate(k):
        return high * fold + lax.rem(low + k, fold)

    first = mine * fold
    below = jnp.maximum(first - 1, 0)
    above = jnp.minimum(first + fold, fold * n_pair - 1)

    def lanes_of(c, n):
        return pl.ds(pl.multiple_of(c * LANES, LANES), n * LANES)

    def greet(o, q):
        pl.semaphore_signal(barrier, inc=1, device_id={"orb": o, "pair": q})

    each_table(greet)
    for j in range(fold):
        for c in range(chips):
            for k in range(1, twin):
                greet(mate(j), lax.rem(chip + c, chips) * twin + lax.rem(core + k, twin))

    loads = [
        pltpu.make_async_copy(send_ref, raw.at[0], load_sem.at[0]),
        pltpu.make_async_copy(left_ref, raw.at[1], load_sem.at[0]),
        pltpu.make_async_copy(off_ref, raw.at[2], load_sem.at[0]),
        pltpu.make_async_copy(orb_ref.at[:, :, lanes_of(first, fold)], slab, load_sem.at[1]),
        pltpu.make_async_copy(orb_ref.at[:, :, lanes_of(below, 1)], edges.at[0], load_sem.at[2]),
        pltpu.make_async_copy(orb_ref.at[:, :, lanes_of(above, 1)], edges.at[1], load_sem.at[2]),
    ]
    for load in loads:
        load.start()

    pltpu.make_async_copy(raw, raw, load_sem.at[0]).wait()
    wide = lax.broadcasted_iota(jnp.int32, (1, LANES), 1)
    sent, left, off = (
        jnp.concatenate([raw[i, 0].astype(f32), jnp.zeros((1, LANES - slots), f32)], axis=1)
        if slots < LANES
        else raw[i, 0].astype(f32)
        for i in range(3)
    )
    dead = left < 0
    table = [
        box_side * 2 * sent,
        jnp.where(dead, DEAD, box_side * 2 * left - off),
        jnp.where(dead, DEAD, 2 * box_side * owned * left + off),
        2 * box_side * owned * sent,
    ]
    for i in range(halves.shape[1]):
        line = jnp.zeros((1, LANES), f32)
        for e in range(i * pack, min((i + 1) * pack, entries)):
            at = (e % pack) * slots
            value = pltpu.roll(table[e % 4], at, 1) if at else table[e % 4]
            line = line + jnp.where(core == e // 4, value, 0.0)
        halves[0, i : i + 1] = line

    loads[3].wait()
    pltpu.make_async_copy(edges, edges, load_sem.at[2]).wait()
    lane = lax.broadcasted_iota(jnp.int32, (box_side, LANES), 1)
    row = lax.broadcasted_iota(jnp.int32, (box_side, LANES), 0)
    for j in range(fold):
        halos = []
        for b in range(owned):
            value = slab[b, :, j * LANES : (j + 1) * LANES].astype(bf16)
            mine_a[j, b] = value
            lower = slab[b, :, (j - 1) * LANES : j * LANES] if j else edges[0, b]
            upper = slab[b, :, (j + 1) * LANES : (j + 2) * LANES] if j + 1 < fold else edges[1, b]
            ends_low = jnp.where(mine > 0, 0, LANES) if j == 0 else 0
            ends_high = jnp.where(mine < n_pair - 1, 0, LANES) if j + 1 == fold else 0
            has_below = lane + ends_low < box_side
            has_above = lane - ends_high >= LANES - box_side
            halo = jnp.where(has_below, pltpu.roll(lower, box_side, 1), 0.0)
            halo = jnp.where(has_above, pltpu.roll(upper, LANES - box_side, 1), halo)
            halos.append(halo if b == 0 else pltpu.roll(halo, b * 2 * box_side, 1))
        mine_a[j, owned] = functools.reduce(jnp.add, halos).astype(bf16)

    pl.semaphore_wait(barrier, n_orb * chips - 1 + fold * chips * (twin - 1))

    def copy_a(o, at):
        return pltpu.make_async_remote_copy(
            src_ref=mine_a.at[lax.rem(o, fold)],
            dst_ref=boxes.at[at],
            send_sem=send_a,
            recv_sem=recv_a.at[at],
            device_id={"orb": o},
        )

    def copy_p(k):
        return pltpu.make_async_remote_copy(
            src_ref=halves.at[0],
            dst_ref=halves.at[k],
            send_sem=send_p.at[k],
            recv_sem=recv_p.at[k],
            device_id={"pair": other_core(k)},
        )

    def copy_i(o, q, from_o, from_q):
        return pltpu.make_async_remote_copy(
            src_ref=tables.at[me * chips + chip],
            dst_ref=tables.at[from_o * chips + from_q // twin],
            send_sem=send_i,
            recv_sem=recv_i,
            device_id={"orb": o, "pair": q},
        )

    def all_of(part, send_sem, recv_sem):
        return pltpu.make_async_remote_copy(
            src_ref=part,
            dst_ref=part,
            send_sem=send_sem,
            recv_sem=recv_sem,
            device_id={"orb": other_orb(1)},
        )

    def block_of(o, q):
        return lax.rem(o, fold) + q * fold

    def copy_d(o, q, from_o, from_q):
        to, at = block_of(o, q), block_of(from_o, from_q)
        return pltpu.make_async_remote_copy(
            src_ref=out_d.at[to],
            dst_ref=out_ref.at[:, lanes_of(at, 1)],
            send_sem=send_d,
            recv_sem=recv_d,
            device_id={"orb": o, "pair": q},
        )

    for k in range(1, twin):
        copy_p(k).start()
    keep_a = pltpu.make_async_copy(mine_a.at[low], boxes.at[me], load_sem.at[0])
    keep_a.start()

    inner = lane % box_side < box_side - 1
    near = lane < LANES - box_side
    not_last = row < box_side - 1
    not_first = row > 0

    def up(v):
        return jnp.where(not_last, pltpu.roll(v, box_side - 1, 0), 0.0)

    def pieces(s, m):
        own = boxes[s, m].astype(f32)
        halo = boxes[s, owned].astype(f32)
        if m:
            halo = pltpu.roll(halo, LANES - m * 2 * box_side, 1)
        after = jnp.where(near, pltpu.roll(own, LANES - box_side, 1), halo)
        return own, after, halo

    def products(s):
        rows = []
        for m in range(owned):
            own, after, halo = pieces(s, m)
            beside = jnp.where(inner, pltpu.roll(own, LANES - 1, 1), 0.0)
            parts = [own * own, own * up(own), own * beside, own * after, own * halo]
            rows.append(jnp.concatenate([p.astype(bf16) for p in parts], axis=1))
        return jnp.concatenate(rows, axis=0)

    at_row = lax.broadcasted_iota(jnp.int32, (side, side), 0)
    at_col = lax.broadcasted_iota(jnp.int32, (side, side), 1)
    key = at_row % box_side - at_col % box_side
    key = key + 2 * box_side * (at_col // box_side) + 2 * box_side * owned * (at_row // box_side)
    key = key.astype(f32)
    use = lax.broadcasted_iota(jnp.int32, (2 * n_pair, LANES), 0)
    use_lane = lax.broadcasted_iota(jnp.int32, (2 * n_pair, LANES), 1)
    use_chip = use % n_pair // twin
    use_given = use % twin * 4 + use // n_pair
    use_own = use_given + 2

    def rows_of(o, entry):
        found = jnp.zeros((2 * n_pair, LANES), f32)
        for c in range(chips):
            for i in range(halves.shape[1]):
                here = (use_chip == c) & (entry // pack == i)
                found = jnp.where(here, tables[o * chips + c, i : i + 1], found)
        return found

    def counts(s, own_tabs):
        given = rows_of(s, use_given)
        found = []
        for j in range(fold):
            codes = jnp.where(use_lane == use_given % pack * slots + mate(j), given, 0.0)
            codes = codes + jnp.where(use_lane == use_own % pack * slots + s, own_tabs[j], 0.0)
            codes = jnp.sum(codes, axis=1, keepdims=True)
            total = jnp.zeros((side, side), f32)
            for u in range(2 * n_pair):
                total = total + jnp.where(key == codes[u : u + 1, :], 1.0, 0.0)
            found.append(total.astype(bf16))
        return jnp.concatenate(found, axis=0)

    for k in range(1, twin):
        copy_p(k).wait_recv()
    tables[me * chips + chip] = functools.reduce(jnp.add, [halves[k] for k in range(twin)])
    each_table(lambda o, q: copy_i(o, q, me, mine).start())
    def send_line(k):
        for j in range(fold):
            copy_a(stripe(k) * fold + lax.rem(low + j, fold), me).start()

    repeat(half, lines, send_line)
    repeat(1, half, send_line)
    for j in range(1, fold):
        copy_a(mate(j), me).start()

    all_tables = all_of(tables.at[pl.ds(0, n_orb * chips - 1)], send_i, recv_i)
    all_tables.wait_recv()
    own_tabs = [rows_of(mate(j), use_own) for j in range(fold)]

    def band(s):
        bands[s] = counts(s, own_tabs)

    repeat(0, n_orb, band)

    def multiply(s):
        return jnp.dot(bands[s], products(s), preferred_element_type=f32)

    keep_a.wait()
    sums[...] = multiply(me)
    for j in range(1, fold):
        copy_a(mate(j), mate(j)).wait_recv()
        sums[...] = sums[...] + multiply(mate(j))

    def process(k):
        for j in range(fold):
            s = stripe(k) * fold + lax.rem(low + j, fold)
            copy_a(s, s).wait_recv()
            sums[...] = sums[...] + multiply(s)

    repeat(1, lines, process)

    scale = -0.25 / 36.0
    for j in reversed(range(fold)):
        fields = []
        for k in range(owned):
            own, after, halo = pieces(mate(j), k)

            def part(i):
                at = j * side + k * box_side
                return sums[at : at + box_side, i * LANES : (i + 1) * LANES]

            c_x, c_z, c_y = part(1), part(2), part(3)
            value = 6.0 * (part(0) * own) + c_x * up(own)
            value = value + jnp.where(not_first, pltpu.roll(c_x * own, 1, 0), 0.0)
            value = value + c_z * pltpu.roll(own, LANES - 1, 1) + pltpu.roll(c_z * own, 1, 1)
            value = value + c_y * after
            flux = pltpu.roll(c_y * own, box_side, 1)
            value = value + jnp.where(lane >= box_side, flux, part(4) * halo)
            fields.append(value * scale)
        for q in range(n_pair):
            at = slice(q * own_rows, (q + 1) * own_rows)
            rows = jnp.concatenate([v[at] for v in fields], axis=0)
            out_d[block_of(mate(j), q)] = rows.astype(bf16)
        repeat(0 if j else 1, n_pair, lambda q: copy_d(mate(j), other_pair(q), me, mine).start())

    keep = pltpu.make_async_copy(
        out_d.at[block_of(me, mine)],
        out_ref.at[:, lanes_of(block_of(me, mine), 1)],
        load_sem.at[0],
    )
    keep.start()
    all_of(boxes.at[pl.ds(0, n_orb - 1)], send_a, send_a).wait_send()
    all_tables.wait_send()
    for k in range(1, twin):
        copy_p(k).wait_send()
    keep.wait()
    all_fields = all_of(out_ref.at[:, lanes_of(0, n_pair * fold - 1)], send_d, recv_d)
    all_fields.wait_recv()
    all_fields.wait_send()


def local(n_orb, n_pair, orbitals, send_index, pair_left, pair_offset):
    owned, box_side, plane = orbitals.shape
    slots = send_index.shape[2]
    own_rows = box_side // n_pair
    fold = plane // n_pair // LANES
    assert owned * 2 * box_side == LANES and slots == n_orb
    assert n_orb % fold == 0 and plane == fold * n_pair * LANES
    twin = 2 if n_pair % 2 == 0 else 1
    lines = -(-4 * twin // (LANES // slots))
    inputs = (orbitals, send_index, pair_left, pair_offset)
    hbm = pl.BlockSpec(memory_space=pltpu.HBM)
    anywhere = pl.BlockSpec(memory_space=pl.ANY)
    dma = pltpu.SemaphoreType.DMA
    field = pl.pallas_call(
        functools.partial(kernel, n_orb, n_pair, fold),
        out_shape=jax.ShapeDtypeStruct((owned * own_rows, plane), bf16),
        in_specs=[hbm] * 4,
        out_specs=anywhere,
        scratch_shapes=[
            pltpu.VMEM((owned, box_side, fold * LANES), f32),
            pltpu.VMEM((2, owned, box_side, LANES), f32),
            pltpu.VMEM((3, 1, 1, slots), jnp.int32),
            pltpu.VMEM((fold, owned + 1, box_side, LANES), bf16),
            pltpu.VMEM((n_orb, owned + 1, box_side, LANES), bf16),
            pltpu.VMEM((fold * owned * box_side, 5 * LANES), f32),
            pltpu.VMEM((twin, lines, LANES), f32),
            pltpu.VMEM((n_orb * n_pair // twin, lines, LANES), f32),
            pltpu.VMEM((n_orb, fold * owned * box_side, owned * box_side), bf16),
            pltpu.VMEM((n_pair * fold, owned * own_rows, LANES), bf16),
            dma((3,)),
            dma,
            dma((n_orb,)),
            dma((twin,)),
            dma((twin,)),
            dma,
            dma,
            dma,
            dma,
        ],
        compiler_params=pltpu.CompilerParams(
            collective_id=0, has_side_effects=True, vmem_limit_bytes=16 << 20
        ),
        name="exchange",
    )(*(pltpu.with_memory_space_constraint(x, pltpu.HBM) for x in inputs))
    return field.astype(f32).reshape(owned, own_rows, plane)


def solution(mesh):
    n_orb, n_pair = mesh.shape["orb"], mesh.shape["pair"]
    return jax.shard_map(
        functools.partial(local, n_orb, n_pair),
        mesh=mesh,
        in_specs=(
            P("orb", None, None),
            P("orb", "pair", None),
            P("orb", "pair", None),
            P("orb", "pair", None),
        ),
        out_specs=P("orb", "pair", None),
        check_vma=False,
    )
```

```python
import functools

import jax
import jax.numpy as jnp
from jax import lax
from jax.experimental import pallas as pl
from jax.experimental.pallas import tpu as pltpu
from jax.sharding import PartitionSpec as P

LANES = 128
DEAD = -10000.0
f32, bf16 = jnp.float32, jnp.bfloat16


def repeat(start, stop, body):
    if stop - start <= 8:
        for k in range(start, stop):
            body(k)
    else:
        lax.fori_loop(start, stop, lambda k, c: (body(k), c)[1], 0)


def kernel(
    n_orb,
    n_pair,
    fold,
    orb_ref,
    send_ref,
    left_ref,
    off_ref,
    out_ref,
    slab,
    edges,
    raw,
    mine_a,
    boxes,
    sums,
    halves,
    tables,
    bands,
    out_d,
    load_sem,
    send_a,
    recv_a,
    send_p,
    recv_p,
    send_i,
    recv_i,
    send_d,
    recv_d,
):
    owned, box_side, plane = orb_ref.shape
    slots = send_ref.shape[2]
    own_rows = box_side // n_pair
    side = owned * box_side
    me = lax.axis_index("orb")
    mine = lax.axis_index("pair")
    lines = n_orb // fold
    high, low = me // fold, lax.rem(me, fold)
    barrier = pltpu.get_barrier_semaphore()

    def other_orb(k):
        return lax.rem(me + k, n_orb)

    def other_pair(k):
        return lax.rem(mine + k, n_pair)

    twin = 2 if n_pair % 2 == 0 else 1
    chips = n_pair // twin
    chip, core = mine // twin, lax.rem(mine, twin)
    entries = 4 * twin
    pack = LANES // slots

    def other_core(k):
        return chip * twin + lax.rem(core + k, twin)

    def same_core(c):
        return lax.rem(chip + c, chips) * twin + core

    def each_table(body):
        for c in reversed(range(chips)):
            repeat(0 if c else 1, n_orb, lambda k: body(other_orb(k), same_core(c)))

    half = lines // 2 if lines % 2 == 0 else lines
    span = lines // half

    def stripe(k):
        return lax.rem(high // half + k // half, span) * half + lax.rem(high + lax.rem(k, half), half)

    def mate(k):
        return high * fold + lax.rem(low + k, fold)

    first = mine * fold
    below = jnp.maximum(first - 1, 0)
    above = jnp.minimum(first + fold, fold * n_pair - 1)

    def lanes_of(c, n):
        return pl.ds(pl.multiple_of(c * LANES, LANES), n * LANES)

    def greet(o, q):
        pl.semaphore_signal(barrier, inc=1, device_id={"orb": o, "pair": q})

    each_table(greet)
    for j in range(fold):
        for c in range(chips):
            for k in range(1, twin):
                greet(mate(j), lax.rem(chip + c, chips) * twin + lax.rem(core + k, twin))

    loads = [
        pltpu.make_async_copy(send_ref, raw.at[0], load_sem.at[0]),
        pltpu.make_async_copy(left_ref, raw.at[1], load_sem.at[0]),
        pltpu.make_async_copy(off_ref, raw.at[2], load_sem.at[0]),
        pltpu.make_async_copy(orb_ref.at[:, :, lanes_of(first, fold)], slab, load_sem.at[1]),
        pltpu.make_async_copy(orb_ref.at[:, :, lanes_of(below, 1)], edges.at[0], load_sem.at[2]),
        pltpu.make_async_copy(orb_ref.at[:, :, lanes_of(above, 1)], edges.at[1], load_sem.at[2]),
    ]
    for load in loads:
        load.start()

    pltpu.make_async_copy(raw, raw, load_sem.at[0]).wait()
    wide = lax.broadcasted_iota(jnp.int32, (1, LANES), 1)
    sent, left, off = (
        jnp.concatenate([raw[i, 0].astype(f32), jnp.zeros((1, LANES - slots), f32)], axis=1)
        if slots < LANES
        else raw[i, 0].astype(f32)
        for i in range(3)
    )
    dead = left < 0
    table = [
        box_side * 2 * sent,
        jnp.where(dead, DEAD, box_side * 2 * left - off),
        jnp.where(dead, DEAD, 2 * box_side * owned * left + off),
        2 * box_side * owned * sent,
    ]
    for i in range(halves.shape[1]):
        line = jnp.zeros((1, LANES), f32)
        for e in range(i * pack, min((i + 1) * pack, entries)):
            at = (e % pack) * slots
            value = pltpu.roll(table[e % 4], at, 1) if at else table[e % 4]
            line = line + jnp.where(core == e // 4, value, 0.0)
        halves[0, i : i + 1] = line

    loads[3].wait()
    pltpu.make_async_copy(edges, edges, load_sem.at[2]).wait()
    lane = lax.broadcasted_iota(jnp.int32, (box_side, LANES), 1)
    row = lax.broadcasted_iota(jnp.int32, (box_side, LANES), 0)
    for j in range(fold):
        halos = []
        for b in range(owned):
            value = slab[b, :, j * LANES : (j + 1) * LANES].astype(bf16)
            mine_a[j, b] = value
            lower = slab[b, :, (j - 1) * LANES : j * LANES] if j else edges[0, b]
            upper = slab[b, :, (j + 1) * LANES : (j + 2) * LANES] if j + 1 < fold else edges[1, b]
            ends_low = jnp.where(mine > 0, 0, LANES) if j == 0 else 0
            ends_high = jnp.where(mine < n_pair - 1, 0, LANES) if j + 1 == fold else 0
            has_below = lane + ends_low < box_side
            has_above = lane - ends_high >= LANES - box_side
            halo = jnp.where(has_below, pltpu.roll(lower, box_side, 1), 0.0)
            halo = jnp.where(has_above, pltpu.roll(upper, LANES - box_side, 1), halo)
            halos.append(halo if b == 0 else pltpu.roll(halo, b * 2 * box_side, 1))
        mine_a[j, owned] = functools.reduce(jnp.add, halos).astype(bf16)

    pl.semaphore_wait(barrier, n_orb * chips - 1 + fold * chips * (twin - 1))

    def copy_a(o, at):
        return pltpu.make_async_remote_copy(
            src_ref=mine_a.at[lax.rem(o, fold)],
            dst_ref=boxes.at[at],
            send_sem=send_a,
            recv_sem=recv_a.at[at],
            device_id={"orb": o},
        )

    def copy_p(k):
        return pltpu.make_async_remote_copy(
            src_ref=halves.at[0],
            dst_ref=halves.at[k],
            send_sem=send_p.at[k],
            recv_sem=recv_p.at[k],
            device_id={"pair": other_core(k)},
        )

    def copy_i(o, q, from_o, from_q):
        return pltpu.make_async_remote_copy(
            src_ref=tables.at[me * chips + chip],
            dst_ref=tables.at[from_o * chips + from_q // twin],
            send_sem=send_i,
            recv_sem=recv_i,
            device_id={"orb": o, "pair": q},
        )

    def all_of(part, send_sem, recv_sem):
        return pltpu.make_async_remote_copy(
            src_ref=part,
            dst_ref=part,
            send_sem=send_sem,
            recv_sem=recv_sem,
            device_id={"orb": other_orb(1)},
        )

    def block_of(o, q):
        return lax.rem(o, fold) + q * fold

    def copy_d(o, q, from_o, from_q):
        to, at = block_of(o, q), block_of(from_o, from_q)
        return pltpu.make_async_remote_copy(
            src_ref=out_d.at[to],
            dst_ref=out_ref.at[:, lanes_of(at, 1)],
            send_sem=send_d,
            recv_sem=recv_d,
            device_id={"orb": o, "pair": q},
        )

    for k in range(1, twin):
        copy_p(k).start()
    keep_a = pltpu.make_async_copy(mine_a.at[low], boxes.at[me], load_sem.at[0])
    keep_a.start()

    inner = lane % box_side < box_side - 1
    near = lane < LANES - box_side
    not_last = row < box_side - 1
    not_first = row > 0

    def up(v):
        return jnp.where(not_last, pltpu.roll(v, box_side - 1, 0), 0.0)

    def pieces(s, m):
        own = boxes[s, m].astype(f32)
        halo = boxes[s, owned].astype(f32)
        if m:
            halo = pltpu.roll(halo, LANES - m * 2 * box_side, 1)
        after = jnp.where(near, pltpu.roll(own, LANES - box_side, 1), halo)
        return own, after, halo

    def products(s):
        rows = []
        for m in range(owned):
            own, after, halo = pieces(s, m)
            beside = jnp.where(inner, pltpu.roll(own, LANES - 1, 1), 0.0)
            parts = [own * own, own * up(own), own * beside, own * after, own * halo]
            rows.append(jnp.concatenate([p.astype(bf16) for p in parts], axis=1))
        return jnp.concatenate(rows, axis=0)

    at_row = lax.broadcasted_iota(jnp.int32, (side, side), 0)
    at_col = lax.broadcasted_iota(jnp.int32, (side, side), 1)
    key = at_row % box_side - at_col % box_side
    key = key + 2 * box_side * (at_col // box_side) + 2 * box_side * owned * (at_row // box_side)
    key = key.astype(f32)
    use = lax.broadcasted_iota(jnp.int32, (2 * n_pair, LANES), 0)
    use_lane = lax.broadcasted_iota(jnp.int32, (2 * n_pair, LANES), 1)
    use_chip = use % n_pair // twin
    use_given = use % twin * 4 + use // n_pair
    use_own = use_given + 2

    def rows_of(o, entry):
        found = jnp.zeros((2 * n_pair, LANES), f32)
        for c in range(chips):
            for i in range(halves.shape[1]):
                here = (use_chip == c) & (entry // pack == i)
                found = jnp.where(here, tables[o * chips + c, i : i + 1], found)
        return found

    def counts(s, own_tabs):
        given = rows_of(s, use_given)
        found = []
        for j in range(fold):
            codes = jnp.where(use_lane == use_given % pack * slots + mate(j), given, 0.0)
            codes = codes + jnp.where(use_lane == use_own % pack * slots + s, own_tabs[j], 0.0)
            codes = jnp.sum(codes, axis=1, keepdims=True)
            total = jnp.zeros((side, side), f32)
            for u in range(2 * n_pair):
                total = total + jnp.where(key == codes[u : u + 1, :], 1.0, 0.0)
            found.append(total.astype(bf16))
        return jnp.concatenate(found, axis=0)

    for k in range(1, twin):
        copy_p(k).wait_recv()
    tables[me * chips + chip] = functools.reduce(jnp.add, [halves[k] for k in range(twin)])
    each_table(lambda o, q: copy_i(o, q, me, mine).start())
    def send_line(k):
        for j in reversed(range(fold)):
            copy_a(stripe(k) * fold + lax.rem(low + j, fold), me).start()

    repeat(half, lines, send_line)
    repeat(1, half, send_line)
    for j in range(1, fold):
        copy_a(mate(j), me).start()

    all_tables = all_of(tables.at[pl.ds(0, n_orb * chips - 1)], send_i, recv_i)
    all_tables.wait_recv()
    own_tabs = [rows_of(mate(j), use_own) for j in range(fold)]

    def band(s):
        bands[s] = counts(s, own_tabs)

    repeat(0, n_orb, band)

    def multiply(s):
        return jnp.dot(bands[s], products(s), preferred_element_type=f32)

    keep_a.wait()
    sums[...] = multiply(me)
    for j in range(1, fold):
        copy_a(mate(j), mate(j)).wait_recv()
        sums[...] = sums[...] + multiply(mate(j))

    def process(k):
        for j in range(fold):
            s = stripe(k) * fold + lax.rem(low + j, fold)
            copy_a(s, s).wait_recv()
            sums[...] = sums[...] + multiply(s)

    repeat(1, lines, process)

    scale = -0.25 / 36.0
    for j in reversed(range(fold)):
        fields = []
        for k in range(owned):
            own, after, halo = pieces(mate(j), k)

            def part(i):
                at = j * side + k * box_side
                return sums[at : at + box_side, i * LANES : (i + 1) * LANES]

            c_x, c_z, c_y = part(1), part(2), part(3)
            value = 6.0 * (part(0) * own) + c_x * up(own)
            value = value + jnp.where(not_first, pltpu.roll(c_x * own, 1, 0), 0.0)
            value = value + c_z * pltpu.roll(own, LANES - 1, 1) + pltpu.roll(c_z * own, 1, 1)
            value = value + c_y * after
            flux = pltpu.roll(c_y * own, box_side, 1)
            value = value + jnp.where(lane >= box_side, flux, part(4) * halo)
            fields.append(value * scale)
        for q in range(n_pair):
            at = slice(q * own_rows, (q + 1) * own_rows)
            rows = jnp.concatenate([v[at] for v in fields], axis=0)
            out_d[block_of(mate(j), q)] = rows.astype(bf16)
        repeat(0 if j else 1, n_pair, lambda q: copy_d(mate(j), other_pair(q), me, mine).start())

    keep = pltpu.make_async_copy(
        out_d.at[block_of(me, mine)],
        out_ref.at[:, lanes_of(block_of(me, mine), 1)],
        load_sem.at[0],
    )
    keep.start()
    all_of(boxes.at[pl.ds(0, n_orb - 1)], send_a, send_a).wait_send()
    all_tables.wait_send()
    for k in range(1, twin):
        copy_p(k).wait_send()
    keep.wait()
    all_fields = all_of(out_ref.at[:, lanes_of(0, n_pair * fold - 1)], send_d, recv_d)
    all_fields.wait_recv()
    all_fields.wait_send()


def local(n_orb, n_pair, orbitals, send_index, pair_left, pair_offset):
    owned, box_side, plane = orbitals.shape
    slots = send_index.shape[2]
    own_rows = box_side // n_pair
    fold = plane // n_pair // LANES
    assert owned * 2 * box_side == LANES and slots == n_orb
    assert n_orb % fold == 0 and plane == fold * n_pair * LANES
    twin = 2 if n_pair % 2 == 0 else 1
    lines = -(-4 * twin // (LANES // slots))
    inputs = (orbitals, send_index, pair_left, pair_offset)
    hbm = pl.BlockSpec(memory_space=pltpu.HBM)
    anywhere = pl.BlockSpec(memory_space=pl.ANY)
    dma = pltpu.SemaphoreType.DMA
    field = pl.pallas_call(
        functools.partial(kernel, n_orb, n_pair, fold),
        out_shape=jax.ShapeDtypeStruct((owned * own_rows, plane), bf16),
        in_specs=[hbm] * 4,
        out_specs=anywhere,
        scratch_shapes=[
            pltpu.VMEM((owned, box_side, fold * LANES), f32),
            pltpu.VMEM((2, owned, box_side, LANES), f32),
            pltpu.VMEM((3, 1, 1, slots), jnp.int32),
            pltpu.VMEM((fold, owned + 1, box_side, LANES), bf16),
            pltpu.VMEM((n_orb, owned + 1, box_side, LANES), bf16),
            pltpu.VMEM((fold * owned * box_side, 5 * LANES), f32),
            pltpu.VMEM((twin, lines, LANES), f32),
            pltpu.VMEM((n_orb * n_pair // twin, lines, LANES), f32),
            pltpu.VMEM((n_orb, fold * owned * box_side, owned * box_side), bf16),
            pltpu.VMEM((n_pair * fold, owned * own_rows, LANES), bf16),
            dma((3,)),
            dma,
            dma((n_orb,)),
            dma((twin,)),
            dma((twin,)),
            dma,
            dma,
            dma,
            dma,
        ],
        compiler_params=pltpu.CompilerParams(
            collective_id=0, has_side_effects=True, vmem_limit_bytes=16 << 20
        ),
        name="exchange",
    )(*(pltpu.with_memory_space_constraint(x, pltpu.HBM) for x in inputs))
    return field.astype(f32).reshape(owned, own_rows, plane)


def solution(mesh):
    n_orb, n_pair = mesh.shape["orb"], mesh.shape["pair"]
    return jax.shard_map(
        functools.partial(local, n_orb, n_pair),
        mesh=mesh,
        in_specs=(
            P("orb", None, None),
            P("orb", "pair", None),
            P("orb", "pair", None),
            P("orb", "pair", None),
        ),
        out_specs=P("orb", "pair", None),
        check_vma=False,
    )
```

```python
import functools

import jax
import jax.numpy as jnp
from jax import lax
from jax.experimental import pallas as pl
from jax.experimental.pallas import tpu as pltpu
from jax.sharding import PartitionSpec as P

LANES = 128
DEAD = -10000.0
f32, bf16 = jnp.float32, jnp.bfloat16


def repeat(start, stop, body):
    if stop - start <= 8:
        for k in range(start, stop):
            body(k)
    else:
        lax.fori_loop(start, stop, lambda k, c: (body(k), c)[1], 0)


def kernel(
    n_orb,
    n_pair,
    fold,
    orb_ref,
    send_ref,
    left_ref,
    off_ref,
    out_ref,
    slab,
    edges,
    raw,
    mine_a,
    boxes,
    sums,
    halves,
    tables,
    bands,
    out_d,
    load_sem,
    send_a,
    recv_a,
    send_p,
    recv_p,
    send_i,
    recv_i,
    send_d,
    recv_d,
):
    owned, box_side, plane = orb_ref.shape
    slots = send_ref.shape[2]
    own_rows = box_side // n_pair
    side = owned * box_side
    me = lax.axis_index("orb")
    mine = lax.axis_index("pair")
    lines = n_orb // fold
    high, low = me // fold, lax.rem(me, fold)
    barrier = pltpu.get_barrier_semaphore()

    def other_orb(k):
        return lax.rem(me + k, n_orb)

    def other_pair(k):
        return lax.rem(mine + k, n_pair)

    twin = 2 if n_pair % 2 == 0 else 1
    chips = n_pair // twin
    chip, core = mine // twin, lax.rem(mine, twin)
    entries = 4 * twin
    pack = LANES // slots

    def other_core(k):
        return chip * twin + lax.rem(core + k, twin)

    def same_core(c):
        return lax.rem(chip + c, chips) * twin + core

    def each_table(body):
        for c in reversed(range(chips)):
            repeat(0 if c else 1, n_orb, lambda k: body(other_orb(k), same_core(c)))

    half = lines // 2 if lines % 2 == 0 else lines
    span = lines // half

    def stripe(k):
        return lax.rem(high // half + k // half, span) * half + lax.rem(high + lax.rem(k, half), half)

    def mate(k):
        return high * fold + lax.rem(low + k, fold)

    first = mine * fold
    below = jnp.maximum(first - 1, 0)
    above = jnp.minimum(first + fold, fold * n_pair - 1)

    def lanes_of(c, n):
        return pl.ds(pl.multiple_of(c * LANES, LANES), n * LANES)

    def greet(o, q):
        pl.semaphore_signal(barrier, inc=1, device_id={"orb": o, "pair": q})

    each_table(greet)
    for j in range(fold):
        for c in range(chips):
            for k in range(1, twin):
                greet(mate(j), lax.rem(chip + c, chips) * twin + lax.rem(core + k, twin))

    loads = [
        pltpu.make_async_copy(send_ref, raw.at[0], load_sem.at[0]),
        pltpu.make_async_copy(left_ref, raw.at[1], load_sem.at[0]),
        pltpu.make_async_copy(off_ref, raw.at[2], load_sem.at[0]),
        pltpu.make_async_copy(orb_ref.at[:, :, lanes_of(first, fold)], slab, load_sem.at[1]),
        pltpu.make_async_copy(orb_ref.at[:, :, lanes_of(below, 1)], edges.at[0], load_sem.at[2]),
        pltpu.make_async_copy(orb_ref.at[:, :, lanes_of(above, 1)], edges.at[1], load_sem.at[2]),
    ]
    for load in loads:
        load.start()

    pltpu.make_async_copy(raw, raw, load_sem.at[0]).wait()
    wide = lax.broadcasted_iota(jnp.int32, (1, LANES), 1)
    sent, left, off = (
        jnp.concatenate([raw[i, 0].astype(f32), jnp.zeros((1, LANES - slots), f32)], axis=1)
        if slots < LANES
        else raw[i, 0].astype(f32)
        for i in range(3)
    )
    dead = left < 0
    table = [
        box_side * 2 * sent,
        jnp.where(dead, DEAD, box_side * 2 * left - off),
        jnp.where(dead, DEAD, 2 * box_side * owned * left + off),
        2 * box_side * owned * sent,
    ]
    for i in range(halves.shape[1]):
        line = jnp.zeros((1, LANES), f32)
        for e in range(i * pack, min((i + 1) * pack, entries)):
            at = (e % pack) * slots
            value = pltpu.roll(table[e % 4], at, 1) if at else table[e % 4]
            line = line + jnp.where(core == e // 4, value, 0.0)
        halves[0, i : i + 1] = line

    loads[3].wait()
    pltpu.make_async_copy(edges, edges, load_sem.at[2]).wait()
    lane = lax.broadcasted_iota(jnp.int32, (box_side, LANES), 1)
    row = lax.broadcasted_iota(jnp.int32, (box_side, LANES), 0)
    for j in range(fold):
        halos = []
        for b in range(owned):
            value = slab[b, :, j * LANES : (j + 1) * LANES].astype(bf16)
            mine_a[j, b] = value
            lower = slab[b, :, (j - 1) * LANES : j * LANES] if j else edges[0, b]
            upper = slab[b, :, (j + 1) * LANES : (j + 2) * LANES] if j + 1 < fold else edges[1, b]
            ends_low = jnp.where(mine > 0, 0, LANES) if j == 0 else 0
            ends_high = jnp.where(mine < n_pair - 1, 0, LANES) if j + 1 == fold else 0
            has_below = lane + ends_low < box_side
            has_above = lane - ends_high >= LANES - box_side
            halo = jnp.where(has_below, pltpu.roll(lower, box_side, 1), 0.0)
            halo = jnp.where(has_above, pltpu.roll(upper, LANES - box_side, 1), halo)
            halos.append(halo if b == 0 else pltpu.roll(halo, b * 2 * box_side, 1))
        mine_a[j, owned] = functools.reduce(jnp.add, halos).astype(bf16)

    pl.semaphore_wait(barrier, n_orb * chips - 1 + fold * chips * (twin - 1))

    def copy_a(o, at):
        return pltpu.make_async_remote_copy(
            src_ref=mine_a.at[lax.rem(o, fold)],
            dst_ref=boxes.at[at],
            send_sem=send_a,
            recv_sem=recv_a.at[at],
            device_id={"orb": o},
        )

    def copy_p(k):
        return pltpu.make_async_remote_copy(
            src_ref=halves.at[0],
            dst_ref=halves.at[k],
            send_sem=send_p.at[k],
            recv_sem=recv_p.at[k],
            device_id={"pair": other_core(k)},
        )

    def copy_i(o, q, from_o, from_q):
        return pltpu.make_async_remote_copy(
            src_ref=tables.at[me * chips + chip],
            dst_ref=tables.at[from_o * chips + from_q // twin],
            send_sem=send_i,
            recv_sem=recv_i,
            device_id={"orb": o, "pair": q},
        )

    def all_of(part, send_sem, recv_sem):
        return pltpu.make_async_remote_copy(
            src_ref=part,
            dst_ref=part,
            send_sem=send_sem,
            recv_sem=recv_sem,
            device_id={"orb": other_orb(1)},
        )

    def block_of(o, q):
        return lax.rem(o, fold) + q * fold

    def copy_d(o, q, from_o, from_q):
        to, at = block_of(o, q), block_of(from_o, from_q)
        return pltpu.make_async_remote_copy(
            src_ref=out_d.at[to],
            dst_ref=out_ref.at[:, lanes_of(at, 1)],
            send_sem=send_d,
            recv_sem=recv_d,
            device_id={"orb": o, "pair": q},
        )

    for k in range(1, twin):
        copy_p(k).start()
    for j in range(1, fold):
        copy_a(mate(j), me).start()
    keep_a = pltpu.make_async_copy(mine_a.at[low], boxes.at[me], load_sem.at[0])
    keep_a.start()

    inner = lane % box_side < box_side - 1
    near = lane < LANES - box_side
    not_last = row < box_side - 1
    not_first = row > 0

    def up(v):
        return jnp.where(not_last, pltpu.roll(v, box_side - 1, 0), 0.0)

    def pieces(s, m):
        own = boxes[s, m].astype(f32)
        halo = boxes[s, owned].astype(f32)
        if m:
            halo = pltpu.roll(halo, LANES - m * 2 * box_side, 1)
        after = jnp.where(near, pltpu.roll(own, LANES - box_side, 1), halo)
        return own, after, halo

    def products(s):
        rows = []
        for m in range(owned):
            own, after, halo = pieces(s, m)
            beside = jnp.where(inner, pltpu.roll(own, LANES - 1, 1), 0.0)
            parts = [own * own, own * up(own), own * beside, own * after, own * halo]
            rows.append(jnp.concatenate([p.astype(bf16) for p in parts], axis=1))
        return jnp.concatenate(rows, axis=0)

    at_row = lax.broadcasted_iota(jnp.int32, (side, side), 0)
    at_col = lax.broadcasted_iota(jnp.int32, (side, side), 1)
    key = at_row % box_side - at_col % box_side
    key = key + 2 * box_side * (at_col // box_side) + 2 * box_side * owned * (at_row // box_side)
    key = key.astype(f32)
    use = lax.broadcasted_iota(jnp.int32, (2 * n_pair, LANES), 0)
    use_lane = lax.broadcasted_iota(jnp.int32, (2 * n_pair, LANES), 1)
    use_chip = use % n_pair // twin
    use_given = use % twin * 4 + use // n_pair
    use_own = use_given + 2

    def rows_of(o, entry):
        found = jnp.zeros((2 * n_pair, LANES), f32)
        for c in range(chips):
            for i in range(halves.shape[1]):
                here = (use_chip == c) & (entry // pack == i)
                found = jnp.where(here, tables[o * chips + c, i : i + 1], found)
        return found

    def counts(s, own_tabs):
        given = rows_of(s, use_given)
        found = []
        for j in range(fold):
            codes = jnp.where(use_lane == use_given % pack * slots + mate(j), given, 0.0)
            codes = codes + jnp.where(use_lane == use_own % pack * slots + s, own_tabs[j], 0.0)
            codes = jnp.sum(codes, axis=1, keepdims=True)
            total = jnp.zeros((side, side), f32)
            for u in range(2 * n_pair):
                total = total + jnp.where(key == codes[u : u + 1, :], 1.0, 0.0)
            found.append(total.astype(bf16))
        return jnp.concatenate(found, axis=0)

    for k in range(1, twin):
        copy_p(k).wait_recv()
    tables[me * chips + chip] = functools.reduce(jnp.add, [halves[k] for k in range(twin)])
    each_table(lambda o, q: copy_i(o, q, me, mine).start())
    def send_line(k):
        for j in reversed(range(fold)):
            copy_a(stripe(k) * fold + lax.rem(low + j, fold), me).start()

    repeat(half, lines, send_line)
    repeat(1, half, send_line)

    all_tables = all_of(tables.at[pl.ds(0, n_orb * chips - 1)], send_i, recv_i)
    all_tables.wait_recv()
    own_tabs = [rows_of(mate(j), use_own) for j in range(fold)]

    def band(s):
        bands[s] = counts(s, own_tabs)

    repeat(0, n_orb, band)

    def multiply(s):
        return jnp.dot(bands[s], products(s), preferred_element_type=f32)

    keep_a.wait()
    sums[...] = multiply(me)
    for j in range(1, fold):
        copy_a(mate(j), mate(j)).wait_recv()
        sums[...] = sums[...] + multiply(mate(j))

    def process(k):
        for j in range(fold):
            s = stripe(k) * fold + lax.rem(low + j, fold)
            copy_a(s, s).wait_recv()
            sums[...] = sums[...] + multiply(s)

    repeat(1, lines, process)

    scale = -0.25 / 36.0
    for j in reversed(range(fold)):
        fields = []
        for k in range(owned):
            own, after, halo = pieces(mate(j), k)

            def part(i):
                at = j * side + k * box_side
                return sums[at : at + box_side, i * LANES : (i + 1) * LANES]

            c_x, c_z, c_y = part(1), part(2), part(3)
            value = 6.0 * (part(0) * own) + c_x * up(own)
            value = value + jnp.where(not_first, pltpu.roll(c_x * own, 1, 0), 0.0)
            value = value + c_z * pltpu.roll(own, LANES - 1, 1) + pltpu.roll(c_z * own, 1, 1)
            value = value + c_y * after
            flux = pltpu.roll(c_y * own, box_side, 1)
            value = value + jnp.where(lane >= box_side, flux, part(4) * halo)
            fields.append(value * scale)
        for q in range(n_pair):
            at = slice(q * own_rows, (q + 1) * own_rows)
            rows = jnp.concatenate([v[at] for v in fields], axis=0)
            out_d[block_of(mate(j), q)] = rows.astype(bf16)
        for c in reversed(range(chips)):
            for k in range(0 if j or c else 1, twin):
                to = lax.rem(chip + c, chips) * twin + lax.rem(core + k, twin)
                copy_d(mate(j), to, me, mine).start()

    keep = pltpu.make_async_copy(
        out_d.at[block_of(me, mine)],
        out_ref.at[:, lanes_of(block_of(me, mine), 1)],
        load_sem.at[0],
    )
    keep.start()
    all_of(boxes.at[pl.ds(0, n_orb - 1)], send_a, send_a).wait_send()
    all_tables.wait_send()
    for k in range(1, twin):
        copy_p(k).wait_send()
    keep.wait()
    all_fields = all_of(out_ref.at[:, lanes_of(0, n_pair * fold - 1)], send_d, recv_d)
    all_fields.wait_recv()
    all_fields.wait_send()


def local(n_orb, n_pair, orbitals, send_index, pair_left, pair_offset):
    owned, box_side, plane = orbitals.shape
    slots = send_index.shape[2]
    own_rows = box_side // n_pair
    fold = plane // n_pair // LANES
    assert owned * 2 * box_side == LANES and slots == n_orb
    assert n_orb % fold == 0 and plane == fold * n_pair * LANES
    twin = 2 if n_pair % 2 == 0 else 1
    lines = -(-4 * twin // (LANES // slots))
    inputs = (orbitals, send_index, pair_left, pair_offset)
    hbm = pl.BlockSpec(memory_space=pltpu.HBM)
    anywhere = pl.BlockSpec(memory_space=pl.ANY)
    dma = pltpu.SemaphoreType.DMA
    field = pl.pallas_call(
        functools.partial(kernel, n_orb, n_pair, fold),
        out_shape=jax.ShapeDtypeStruct((owned * own_rows, plane), bf16),
        in_specs=[hbm] * 4,
        out_specs=anywhere,
        scratch_shapes=[
            pltpu.VMEM((owned, box_side, fold * LANES), f32),
            pltpu.VMEM((2, owned, box_side, LANES), f32),
            pltpu.VMEM((3, 1, 1, slots), jnp.int32),
            pltpu.VMEM((fold, owned + 1, box_side, LANES), bf16),
            pltpu.VMEM((n_orb, owned + 1, box_side, LANES), bf16),
            pltpu.VMEM((fold * owned * box_side, 5 * LANES), f32),
            pltpu.VMEM((twin, lines, LANES), f32),
            pltpu.VMEM((n_orb * n_pair // twin, lines, LANES), f32),
            pltpu.VMEM((n_orb, fold * owned * box_side, owned * box_side), bf16),
            pltpu.VMEM((n_pair * fold, owned * own_rows, LANES), bf16),
            dma((3,)),
            dma,
            dma((n_orb,)),
            dma((twin,)),
            dma((twin,)),
            dma,
            dma,
            dma,
            dma,
        ],
        compiler_params=pltpu.CompilerParams(
            collective_id=0, has_side_effects=True, vmem_limit_bytes=16 << 20
        ),
        name="exchange",
    )(*(pltpu.with_memory_space_constraint(x, pltpu.HBM) for x in inputs))
    return field.astype(f32).reshape(owned, own_rows, plane)


def solution(mesh):
    n_orb, n_pair = mesh.shape["orb"], mesh.shape["pair"]
    return jax.shard_map(
        functools.partial(local, n_orb, n_pair),
        mesh=mesh,
        in_specs=(
            P("orb", None, None),
            P("orb", "pair", None),
            P("orb", "pair", None),
            P("orb", "pair", None),
        ),
        out_specs=P("orb", "pair", None),
        check_vma=False,
    )
```

```python
import functools

import jax
import jax.numpy as jnp
from jax import lax
from jax.experimental import pallas as pl
from jax.experimental.pallas import tpu as pltpu
from jax.sharding import PartitionSpec as P

LANES = 128
DEAD = -10000.0
f32, bf16 = jnp.float32, jnp.bfloat16


def repeat(start, stop, body):
    if stop - start <= 8:
        for k in range(start, stop):
            body(k)
    else:
        lax.fori_loop(start, stop, lambda k, c: (body(k), c)[1], 0)


def kernel(
    n_orb,
    n_pair,
    fold,
    orb_ref,
    send_ref,
    left_ref,
    off_ref,
    out_ref,
    slab,
    edges,
    raw,
    mine_a,
    boxes,
    sums,
    halves,
    tables,
    bands,
    out_d,
    load_sem,
    send_a,
    recv_a,
    send_p,
    recv_p,
    send_i,
    recv_i,
    send_d,
    recv_d,
):
    owned, box_side, plane = orb_ref.shape
    slots = send_ref.shape[2]
    own_rows = box_side // n_pair
    side = owned * box_side
    me = lax.axis_index("orb")
    mine = lax.axis_index("pair")
    lines = n_orb // fold
    high, low = me // fold, lax.rem(me, fold)
    barrier = pltpu.get_barrier_semaphore()

    def other_orb(k):
        return lax.rem(me + k, n_orb)

    def other_pair(k):
        return lax.rem(mine + k, n_pair)

    twin = 2 if n_pair % 2 == 0 else 1
    chips = n_pair // twin
    chip, core = mine // twin, lax.rem(mine, twin)
    entries = 4 * twin
    pack = LANES // slots

    def other_core(k):
        return chip * twin + lax.rem(core + k, twin)

    def same_core(c):
        return lax.rem(chip + c, chips) * twin + core

    def each_table(body):
        for c in reversed(range(chips)):
            repeat(0 if c else 1, n_orb, lambda k: body(other_orb(k), same_core(c)))

    half = lines // 2 if lines % 2 == 0 else lines
    span = lines // half

    def stripe(k):
        return lax.rem(high // half + k // half, span) * half + lax.rem(high + lax.rem(k, half), half)

    def mate(k):
        return high * fold + lax.rem(low + k, fold)

    first = mine * fold
    below = jnp.maximum(first - 1, 0)
    above = jnp.minimum(first + fold, fold * n_pair - 1)

    def lanes_of(c, n):
        return pl.ds(pl.multiple_of(c * LANES, LANES), n * LANES)

    def greet(o, q):
        pl.semaphore_signal(barrier, inc=1, device_id={"orb": o, "pair": q})

    each_table(greet)
    for j in range(fold):
        for c in range(chips):
            for k in range(1, twin):
                greet(mate(j), lax.rem(chip + c, chips) * twin + lax.rem(core + k, twin))

    loads = [
        pltpu.make_async_copy(send_ref, raw.at[0], load_sem.at[0]),
        pltpu.make_async_copy(left_ref, raw.at[1], load_sem.at[0]),
        pltpu.make_async_copy(off_ref, raw.at[2], load_sem.at[0]),
        pltpu.make_async_copy(orb_ref.at[:, :, lanes_of(first, fold)], slab, load_sem.at[1]),
        pltpu.make_async_copy(orb_ref.at[:, :, lanes_of(below, 1)], edges.at[0], load_sem.at[2]),
        pltpu.make_async_copy(orb_ref.at[:, :, lanes_of(above, 1)], edges.at[1], load_sem.at[2]),
    ]
    for load in loads:
        load.start()

    pltpu.make_async_copy(raw, raw, load_sem.at[0]).wait()
    wide = lax.broadcasted_iota(jnp.int32, (1, LANES), 1)
    sent, left, off = (
        jnp.concatenate([raw[i, 0].astype(f32), jnp.zeros((1, LANES - slots), f32)], axis=1)
        if slots < LANES
        else raw[i, 0].astype(f32)
        for i in range(3)
    )
    dead = left < 0
    table = [
        box_side * 2 * sent,
        jnp.where(dead, DEAD, box_side * 2 * left - off),
        jnp.where(dead, DEAD, 2 * box_side * owned * left + off),
        2 * box_side * owned * sent,
    ]
    for i in range(halves.shape[1]):
        line = jnp.zeros((1, LANES), f32)
        for e in range(i * pack, min((i + 1) * pack, entries)):
            at = (e % pack) * slots
            value = pltpu.roll(table[e % 4], at, 1) if at else table[e % 4]
            line = line + jnp.where(core == e // 4, value, 0.0)
        halves[0, i : i + 1] = line

    loads[3].wait()
    pltpu.make_async_copy(edges, edges, load_sem.at[2]).wait()
    lane = lax.broadcasted_iota(jnp.int32, (box_side, LANES), 1)
    row = lax.broadcasted_iota(jnp.int32, (box_side, LANES), 0)
    for j in range(fold):
        halos = []
        for b in range(owned):
            value = slab[b, :, j * LANES : (j + 1) * LANES].astype(bf16)
            mine_a[j, b] = value
            lower = slab[b, :, (j - 1) * LANES : j * LANES] if j else edges[0, b]
            upper = slab[b, :, (j + 1) * LANES : (j + 2) * LANES] if j + 1 < fold else edges[1, b]
            ends_low = jnp.where(mine > 0, 0, LANES) if j == 0 else 0
            ends_high = jnp.where(mine < n_pair - 1, 0, LANES) if j + 1 == fold else 0
            has_below = lane + ends_low < box_side
            has_above = lane - ends_high >= LANES - box_side
            halo = jnp.where(has_below, pltpu.roll(lower, box_side, 1), 0.0)
            halo = jnp.where(has_above, pltpu.roll(upper, LANES - box_side, 1), halo)
            halos.append(halo if b == 0 else pltpu.roll(halo, b * 2 * box_side, 1))
        mine_a[j, owned] = functools.reduce(jnp.add, halos).astype(bf16)

    boxes[me] = mine_a[low]
    pl.semaphore_wait(barrier, n_orb * chips - 1 + fold * chips * (twin - 1))

    def copy_a(o, at):
        return pltpu.make_async_remote_copy(
            src_ref=mine_a.at[lax.rem(o, fold)],
            dst_ref=boxes.at[at],
            send_sem=send_a,
            recv_sem=recv_a.at[at],
            device_id={"orb": o},
        )

    def copy_p(k):
        return pltpu.make_async_remote_copy(
            src_ref=halves.at[0],
            dst_ref=halves.at[k],
            send_sem=send_p.at[k],
            recv_sem=recv_p.at[k],
            device_id={"pair": other_core(k)},
        )

    def copy_i(o, q, from_o, from_q):
        return pltpu.make_async_remote_copy(
            src_ref=tables.at[me * chips + chip],
            dst_ref=tables.at[from_o * chips + from_q // twin],
            send_sem=send_i,
            recv_sem=recv_i,
            device_id={"orb": o, "pair": q},
        )

    def all_of(part, send_sem, recv_sem):
        return pltpu.make_async_remote_copy(
            src_ref=part,
            dst_ref=part,
            send_sem=send_sem,
            recv_sem=recv_sem,
            device_id={"orb": other_orb(1)},
        )

    def block_of(o, q):
        return lax.rem(o, fold) + q * fold

    def copy_d(o, q, from_o, from_q):
        to, at = block_of(o, q), block_of(from_o, from_q)
        return pltpu.make_async_remote_copy(
            src_ref=out_d.at[to],
            dst_ref=out_ref.at[:, lanes_of(at, 1)],
            send_sem=send_d,
            recv_sem=recv_d,
            device_id={"orb": o, "pair": q},
        )

    for k in range(1, twin):
        copy_p(k).start()
    for j in range(1, fold):
        copy_a(mate(j), me).start()

    inner = lane % box_side < box_side - 1
    near = lane < LANES - box_side
    not_last = row < box_side - 1
    not_first = row > 0

    def up(v):
        return jnp.where(not_last, pltpu.roll(v, box_side - 1, 0), 0.0)

    def pieces(s, m):
        own = boxes[s, m].astype(f32)
        halo = boxes[s, owned].astype(f32)
        if m:
            halo = pltpu.roll(halo, LANES - m * 2 * box_side, 1)
        after = jnp.where(near, pltpu.roll(own, LANES - box_side, 1), halo)
        return own, after, halo

    def products(s):
        rows = []
        for m in range(owned):
            own, after, halo = pieces(s, m)
            beside = jnp.where(inner, pltpu.roll(own, LANES - 1, 1), 0.0)
            parts = [own * own, own * up(own), own * beside, own * after, own * halo]
            rows.append(jnp.concatenate([p.astype(bf16) for p in parts], axis=1))
        return jnp.concatenate(rows, axis=0)

    at_row = lax.broadcasted_iota(jnp.int32, (side, side), 0)
    at_col = lax.broadcasted_iota(jnp.int32, (side, side), 1)
    key = at_row % box_side - at_col % box_side
    key = key + 2 * box_side * (at_col // box_side) + 2 * box_side * owned * (at_row // box_side)
    key = key.astype(f32)
    use = lax.broadcasted_iota(jnp.int32, (2 * n_pair, LANES), 0)
    use_lane = lax.broadcasted_iota(jnp.int32, (2 * n_pair, LANES), 1)
    use_chip = use % n_pair // twin
    use_given = use % twin * 4 + use // n_pair
    use_own = use_given + 2

    def rows_of(o, entry):
        found = jnp.zeros((2 * n_pair, LANES), f32)
        for c in range(chips):
            for i in range(halves.shape[1]):
                here = (use_chip == c) & (entry // pack == i)
                found = jnp.where(here, tables[o * chips + c, i : i + 1], found)
        return found

    def counts(s, own_tabs):
        given = rows_of(s, use_given)
        found = []
        for j in range(fold):
            codes = jnp.where(use_lane == use_given % pack * slots + mate(j), given, 0.0)
            codes = codes + jnp.where(use_lane == use_own % pack * slots + s, own_tabs[j], 0.0)
            codes = jnp.sum(codes, axis=1, keepdims=True)
            total = jnp.zeros((side, side), f32)
            for u in range(2 * n_pair):
                total = total + jnp.where(key == codes[u : u + 1, :], 1.0, 0.0)
            found.append(total.astype(bf16))
        return jnp.concatenate(found, axis=0)

    for k in range(1, twin):
        copy_p(k).wait_recv()
    tables[me * chips + chip] = functools.reduce(jnp.add, [halves[k] for k in range(twin)])
    each_table(lambda o, q: copy_i(o, q, me, mine).start())
    def send_line(k):
        for j in reversed(range(fold)):
            copy_a(stripe(k) * fold + lax.rem(low + j, fold), me).start()

    repeat(half, lines, send_line)
    repeat(1, half, send_line)

    all_tables = all_of(tables.at[pl.ds(0, n_orb * chips - 1)], send_i, recv_i)
    all_tables.wait_recv()
    own_tabs = [rows_of(mate(j), use_own) for j in range(fold)]

    def band(s):
        bands[s] = counts(s, own_tabs)

    repeat(0, n_orb, band)

    def multiply(s):
        return jnp.dot(bands[s], products(s), preferred_element_type=f32)

    sums[...] = multiply(me)
    for j in range(1, fold):
        copy_a(mate(j), mate(j)).wait_recv()
        sums[...] = sums[...] + multiply(mate(j))

    def process(k):
        for j in range(fold):
            s = stripe(k) * fold + lax.rem(low + j, fold)
            copy_a(s, s).wait_recv()
            sums[...] = sums[...] + multiply(s)

    repeat(1, lines, process)

    scale = -0.25 / 36.0
    for j in reversed(range(fold)):
        fields = []
        for k in range(owned):
            own, after, halo = pieces(mate(j), k)

            def part(i):
                at = j * side + k * box_side
                return sums[at : at + box_side, i * LANES : (i + 1) * LANES]

            c_x, c_z, c_y = part(1), part(2), part(3)
            value = 6.0 * (part(0) * own) + c_x * up(own)
            value = value + jnp.where(not_first, pltpu.roll(c_x * own, 1, 0), 0.0)
            value = value + c_z * pltpu.roll(own, LANES - 1, 1) + pltpu.roll(c_z * own, 1, 1)
            value = value + c_y * after
            flux = pltpu.roll(c_y * own, box_side, 1)
            value = value + jnp.where(lane >= box_side, flux, part(4) * halo)
            fields.append(value * scale)
        for q in range(n_pair):
            at = slice(q * own_rows, (q + 1) * own_rows)
            rows = jnp.concatenate([v[at] for v in fields], axis=0)
            out_d[block_of(mate(j), q)] = rows.astype(bf16)
        for c in reversed(range(chips)):
            for k in range(0 if j or c else 1, twin):
                to = lax.rem(chip + c, chips) * twin + lax.rem(core + k, twin)
                copy_d(mate(j), to, me, mine).start()

    keep = pltpu.make_async_copy(
        out_d.at[block_of(me, mine)],
        out_ref.at[:, lanes_of(block_of(me, mine), 1)],
        load_sem.at[0],
    )
    keep.start()
    all_of(boxes.at[pl.ds(0, n_orb - 1)], send_a, send_a).wait_send()
    all_tables.wait_send()
    for k in range(1, twin):
        copy_p(k).wait_send()
    keep.wait()
    all_fields = all_of(out_ref.at[:, lanes_of(0, n_pair * fold - 1)], send_d, recv_d)
    all_fields.wait_recv()
    all_fields.wait_send()


def local(n_orb, n_pair, orbitals, send_index, pair_left, pair_offset):
    owned, box_side, plane = orbitals.shape
    slots = send_index.shape[2]
    own_rows = box_side // n_pair
    fold = plane // n_pair // LANES
    assert owned * 2 * box_side == LANES and slots == n_orb
    assert n_orb % fold == 0 and plane == fold * n_pair * LANES
    twin = 2 if n_pair % 2 == 0 else 1
    lines = -(-4 * twin // (LANES // slots))
    inputs = (orbitals, send_index, pair_left, pair_offset)
    hbm = pl.BlockSpec(memory_space=pltpu.HBM)
    anywhere = pl.BlockSpec(memory_space=pl.ANY)
    dma = pltpu.SemaphoreType.DMA
    field = pl.pallas_call(
        functools.partial(kernel, n_orb, n_pair, fold),
        out_shape=jax.ShapeDtypeStruct((owned * own_rows, plane), bf16),
        in_specs=[hbm] * 4,
        out_specs=anywhere,
        scratch_shapes=[
            pltpu.VMEM((owned, box_side, fold * LANES), f32),
            pltpu.VMEM((2, owned, box_side, LANES), f32),
            pltpu.VMEM((3, 1, 1, slots), jnp.int32),
            pltpu.VMEM((fold, owned + 1, box_side, LANES), bf16),
            pltpu.VMEM((n_orb, owned + 1, box_side, LANES), bf16),
            pltpu.VMEM((fold * owned * box_side, 5 * LANES), f32),
            pltpu.VMEM((twin, lines, LANES), f32),
            pltpu.VMEM((n_orb * n_pair // twin, lines, LANES), f32),
            pltpu.VMEM((n_orb, fold * owned * box_side, owned * box_side), bf16),
            pltpu.VMEM((n_pair * fold, owned * own_rows, LANES), bf16),
            dma((3,)),
            dma,
            dma((n_orb,)),
            dma((twin,)),
            dma((twin,)),
            dma,
            dma,
            dma,
            dma,
        ],
        compiler_params=pltpu.CompilerParams(
            collective_id=0, has_side_effects=True, vmem_limit_bytes=16 << 20
        ),
        name="exchange",
    )(*(pltpu.with_memory_space_constraint(x, pltpu.HBM) for x in inputs))
    return field.astype(f32).reshape(owned, own_rows, plane)


def solution(mesh):
    n_orb, n_pair = mesh.shape["orb"], mesh.shape["pair"]
    return jax.shard_map(
        functools.partial(local, n_orb, n_pair),
        mesh=mesh,
        in_specs=(
            P("orb", None, None),
            P("orb", "pair", None),
            P("orb", "pair", None),
            P("orb", "pair", None),
        ),
        out_specs=P("orb", "pair", None),
        check_vma=False,
    )
```

```python
import functools

import jax
import jax.numpy as jnp
from jax import lax
from jax.experimental import pallas as pl
from jax.experimental.pallas import tpu as pltpu
from jax.sharding import PartitionSpec as P

LANES = 128
DEAD = -10000.0
f32, bf16 = jnp.float32, jnp.bfloat16


def repeat(start, stop, body):
    if stop - start <= 8:
        for k in range(start, stop):
            body(k)
    else:
        lax.fori_loop(start, stop, lambda k, c: (body(k), c)[1], 0)


def kernel(
    n_orb,
    n_pair,
    fold,
    orb_ref,
    send_ref,
    left_ref,
    off_ref,
    out_ref,
    slab,
    edges,
    raw,
    mine_a,
    boxes,
    sums,
    halves,
    tables,
    bands,
    out_d,
    load_sem,
    send_a,
    recv_a,
    send_p,
    recv_p,
    send_i,
    recv_i,
    send_d,
    recv_d,
):
    owned, box_side, plane = orb_ref.shape
    slots = send_ref.shape[2]
    own_rows = box_side // n_pair
    side = owned * box_side
    me = lax.axis_index("orb")
    mine = lax.axis_index("pair")
    lines = n_orb // fold
    high, low = me // fold, lax.rem(me, fold)
    barrier = pltpu.get_barrier_semaphore()

    def other_orb(k):
        return lax.rem(me + k, n_orb)

    def other_pair(k):
        return lax.rem(mine + k, n_pair)

    twin = 2 if n_pair % 2 == 0 else 1
    chips = n_pair // twin
    chip, core = mine // twin, lax.rem(mine, twin)
    entries = 4 * twin
    pack = LANES // slots

    def other_core(k):
        return chip * twin + lax.rem(core + k, twin)

    def same_core(c):
        return lax.rem(chip + c, chips) * twin + core

    def each_table(body):
        for c in reversed(range(chips)):
            repeat(0 if c else 1, n_orb, lambda k: body(other_orb(k), same_core(c)))

    half = lines // 2 if lines % 2 == 0 else lines
    span = lines // half

    def stripe(k):
        return lax.rem(high // half + k // half, span) * half + lax.rem(high + lax.rem(k, half), half)

    def mate(k):
        return high * fold + lax.rem(low + k, fold)

    first = mine * fold
    below = jnp.maximum(first - 1, 0)
    above = jnp.minimum(first + fold, fold * n_pair - 1)

    def lanes_of(c, n):
        return pl.ds(pl.multiple_of(c * LANES, LANES), n * LANES)

    def greet(o, q):
        pl.semaphore_signal(barrier, inc=1, device_id={"orb": o, "pair": q})

    each_table(greet)
    for j in range(fold):
        for c in range(chips):
            for k in range(1, twin):
                greet(mate(j), lax.rem(chip + c, chips) * twin + lax.rem(core + k, twin))

    loads = [
        pltpu.make_async_copy(send_ref, raw.at[0], load_sem.at[0]),
        pltpu.make_async_copy(left_ref, raw.at[1], load_sem.at[0]),
        pltpu.make_async_copy(off_ref, raw.at[2], load_sem.at[0]),
        pltpu.make_async_copy(orb_ref.at[:, :, lanes_of(first, fold)], slab, load_sem.at[1]),
        pltpu.make_async_copy(orb_ref.at[:, :, lanes_of(below, 1)], edges.at[0], load_sem.at[2]),
        pltpu.make_async_copy(orb_ref.at[:, :, lanes_of(above, 1)], edges.at[1], load_sem.at[2]),
    ]
    for load in loads:
        load.start()

    pltpu.make_async_copy(raw, raw, load_sem.at[0]).wait()
    wide = lax.broadcasted_iota(jnp.int32, (1, LANES), 1)
    sent, left, off = (
        jnp.concatenate([raw[i, 0].astype(f32), jnp.zeros((1, LANES - slots), f32)], axis=1)
        if slots < LANES
        else raw[i, 0].astype(f32)
        for i in range(3)
    )
    dead = left < 0
    table = [
        box_side * 2 * sent,
        jnp.where(dead, DEAD, box_side * 2 * left - off),
        jnp.where(dead, DEAD, 2 * box_side * owned * left + off),
        2 * box_side * owned * sent,
    ]
    for i in range(halves.shape[1]):
        line = jnp.zeros((1, LANES), f32)
        for e in range(i * pack, min((i + 1) * pack, entries)):
            at = (e % pack) * slots
            value = pltpu.roll(table[e % 4], at, 1) if at else table[e % 4]
            line = line + jnp.where(core == e // 4, value, 0.0)
        halves[0, i : i + 1] = line

    loads[3].wait()
    pltpu.make_async_copy(edges, edges, load_sem.at[2]).wait()
    lane = lax.broadcasted_iota(jnp.int32, (box_side, LANES), 1)
    row = lax.broadcasted_iota(jnp.int32, (box_side, LANES), 0)
    for j in range(fold):
        halos = []
        for b in range(owned):
            value = slab[b, :, j * LANES : (j + 1) * LANES].astype(bf16)
            mine_a[j, b] = value
            lower = slab[b, :, (j - 1) * LANES : j * LANES] if j else edges[0, b]
            upper = slab[b, :, (j + 1) * LANES : (j + 2) * LANES] if j + 1 < fold else edges[1, b]
            ends_low = jnp.where(mine > 0, 0, LANES) if j == 0 else 0
            ends_high = jnp.where(mine < n_pair - 1, 0, LANES) if j + 1 == fold else 0
            has_below = lane + ends_low < box_side
            has_above = lane - ends_high >= LANES - box_side
            halo = jnp.where(has_below, pltpu.roll(lower, box_side, 1), 0.0)
            halo = jnp.where(has_above, pltpu.roll(upper, LANES - box_side, 1), halo)
            halos.append(halo if b == 0 else pltpu.roll(halo, b * 2 * box_side, 1))
        mine_a[j, owned] = functools.reduce(jnp.add, halos).astype(bf16)

    pl.semaphore_wait(barrier, n_orb * chips - 1 + fold * chips * (twin - 1))

    def copy_a(o, at):
        return pltpu.make_async_remote_copy(
            src_ref=mine_a.at[lax.rem(o, fold)],
            dst_ref=boxes.at[at],
            send_sem=send_a,
            recv_sem=recv_a.at[at],
            device_id={"orb": o},
        )

    def copy_p(k):
        return pltpu.make_async_remote_copy(
            src_ref=halves.at[0],
            dst_ref=halves.at[k],
            send_sem=send_p.at[k],
            recv_sem=recv_p.at[k],
            device_id={"pair": other_core(k)},
        )

    def copy_i(o, q, from_o, from_q):
        return pltpu.make_async_remote_copy(
            src_ref=tables.at[me * chips + chip],
            dst_ref=tables.at[from_o * chips + from_q // twin],
            send_sem=send_i,
            recv_sem=recv_i,
            device_id={"orb": o, "pair": q},
        )

    def all_of(part, send_sem, recv_sem):
        return pltpu.make_async_remote_copy(
            src_ref=part,
            dst_ref=part,
            send_sem=send_sem,
            recv_sem=recv_sem,
            device_id={"orb": other_orb(1)},
        )

    def block_of(o, q):
        return lax.rem(o, fold) + q * fold

    def copy_d(o, q, from_o, from_q):
        to, at = block_of(o, q), block_of(from_o, from_q)
        return pltpu.make_async_remote_copy(
            src_ref=out_d.at[to],
            dst_ref=out_ref.at[:, lanes_of(at, 1)],
            send_sem=send_d,
            recv_sem=recv_d,
            device_id={"orb": o, "pair": q},
        )

    for k in range(1, twin):
        copy_p(k).start()
    for j in range(1, fold):
        copy_a(mate(j), me).start()
    keep_a = pltpu.make_async_copy(mine_a.at[low], boxes.at[me], load_sem.at[0])
    keep_a.start()

    inner = lane % box_side < box_side - 1
    near = lane < LANES - box_side
    not_last = row < box_side - 1
    not_first = row > 0

    def up(v):
        return jnp.where(not_last, pltpu.roll(v, box_side - 1, 0), 0.0)

    def pieces(s, m):
        own = boxes[s, m].astype(f32)
        halo = boxes[s, owned].astype(f32)
        if m:
            halo = pltpu.roll(halo, LANES - m * 2 * box_side, 1)
        after = jnp.where(near, pltpu.roll(own, LANES - box_side, 1), halo)
        return own, after, halo

    def products(s):
        rows = []
        for m in range(owned):
            own, after, halo = pieces(s, m)
            beside = jnp.where(inner, pltpu.roll(own, LANES - 1, 1), 0.0)
            parts = [own * own, own * up(own), own * beside, own * after, own * halo]
            rows.append(jnp.concatenate([p.astype(bf16) for p in parts], axis=1))
        return jnp.concatenate(rows, axis=0)

    at_row = lax.broadcasted_iota(jnp.int32, (side, side), 0)
    at_col = lax.broadcasted_iota(jnp.int32, (side, side), 1)
    key = at_row % box_side - at_col % box_side
    key = key + 2 * box_side * (at_col // box_side) + 2 * box_side * owned * (at_row // box_side)
    key = key.astype(f32)
    use = lax.broadcasted_iota(jnp.int32, (2 * n_pair, LANES), 0)
    use_lane = lax.broadcasted_iota(jnp.int32, (2 * n_pair, LANES), 1)
    use_chip = use % n_pair // twin
    use_given = use % twin * 4 + use // n_pair
    use_own = use_given + 2

    def rows_of(o, entry):
        found = jnp.zeros((2 * n_pair, LANES), f32)
        for c in range(chips):
            for i in range(halves.shape[1]):
                here = (use_chip == c) & (entry // pack == i)
                found = jnp.where(here, tables[o * chips + c, i : i + 1], found)
        return found

    def counts(s, own_tabs):
        given = rows_of(s, use_given)
        found = []
        for j in range(fold):
            codes = jnp.where(use_lane == use_given % pack * slots + mate(j), given, 0.0)
            codes = codes + jnp.where(use_lane == use_own % pack * slots + s, own_tabs[j], 0.0)
            codes = jnp.sum(codes, axis=1, keepdims=True)
            total = jnp.zeros((side, side), f32)
            for u in range(2 * n_pair):
                total = total + jnp.where(key == codes[u : u + 1, :], 1.0, 0.0)
            found.append(total.astype(bf16))
        return jnp.concatenate(found, axis=0)

    for k in range(1, twin):
        copy_p(k).wait_recv()
    tables[me * chips + chip] = functools.reduce(jnp.add, [halves[k] for k in range(twin)])
    def tables_to(k, c):
        for j in reversed(range(fold)):
            copy_i(stripe(k) * fold + lax.rem(low + j, fold), same_core(c), me, mine).start()

    for c in reversed(range(chips)):
        repeat(half, lines, functools.partial(tables_to, c=c))
    for c in reversed(range(chips)):
        repeat(1, half, functools.partial(tables_to, c=c))
        for j in range(0 if c else 1, fold):
            copy_i(mate(j), same_core(c), me, mine).start()
    def send_line(k):
        for j in reversed(range(fold)):
            copy_a(stripe(k) * fold + lax.rem(low + j, fold), me).start()

    repeat(half, lines, send_line)
    repeat(1, half, send_line)

    all_tables = all_of(tables.at[pl.ds(0, n_orb * chips - 1)], send_i, recv_i)
    all_tables.wait_recv()
    own_tabs = [rows_of(mate(j), use_own) for j in range(fold)]

    def band(s):
        bands[s] = counts(s, own_tabs)

    repeat(0, n_orb, band)

    def multiply(s):
        return jnp.dot(bands[s], products(s), preferred_element_type=f32)

    keep_a.wait()
    sums[...] = multiply(me)
    for j in range(1, fold):
        copy_a(mate(j), mate(j)).wait_recv()
        sums[...] = sums[...] + multiply(mate(j))

    def process(k):
        for j in range(fold):
            s = stripe(k) * fold + lax.rem(low + j, fold)
            copy_a(s, s).wait_recv()
            sums[...] = sums[...] + multiply(s)

    repeat(1, lines, process)

    scale = -0.25 / 36.0
    for j in reversed(range(fold)):
        fields = []
        for k in range(owned):
            own, after, halo = pieces(mate(j), k)

            def part(i):
                at = j * side + k * box_side
                return sums[at : at + box_side, i * LANES : (i + 1) * LANES]

            c_x, c_z, c_y = part(1), part(2), part(3)
            value = 6.0 * (part(0) * own) + c_x * up(own)
            value = value + jnp.where(not_first, pltpu.roll(c_x * own, 1, 0), 0.0)
            value = value + c_z * pltpu.roll(own, LANES - 1, 1) + pltpu.roll(c_z * own, 1, 1)
            value = value + c_y * after
            flux = pltpu.roll(c_y * own, box_side, 1)
            value = value + jnp.where(lane >= box_side, flux, part(4) * halo)
            fields.append(value * scale)
        for q in range(n_pair):
            at = slice(q * own_rows, (q + 1) * own_rows)
            rows = jnp.concatenate([v[at] for v in fields], axis=0)
            out_d[block_of(mate(j), q)] = rows.astype(bf16)
        for c in reversed(range(chips)):
            for k in range(0 if j or c else 1, twin):
                to = lax.rem(chip + c, chips) * twin + lax.rem(core + k, twin)
                copy_d(mate(j), to, me, mine).start()

    keep = pltpu.make_async_copy(
        out_d.at[block_of(me, mine)],
        out_ref.at[:, lanes_of(block_of(me, mine), 1)],
        load_sem.at[0],
    )
    keep.start()
    all_of(boxes.at[pl.ds(0, n_orb - 1)], send_a, send_a).wait_send()
    all_tables.wait_send()
    for k in range(1, twin):
        copy_p(k).wait_send()
    keep.wait()
    all_fields = all_of(out_ref.at[:, lanes_of(0, n_pair * fold - 1)], send_d, recv_d)
    all_fields.wait_recv()
    all_fields.wait_send()


def local(n_orb, n_pair, orbitals, send_index, pair_left, pair_offset):
    owned, box_side, plane = orbitals.shape
    slots = send_index.shape[2]
    own_rows = box_side // n_pair
    fold = plane // n_pair // LANES
    assert owned * 2 * box_side == LANES and slots == n_orb
    assert n_orb % fold == 0 and plane == fold * n_pair * LANES
    twin = 2 if n_pair % 2 == 0 else 1
    lines = -(-4 * twin // (LANES // slots))
    inputs = (orbitals, send_index, pair_left, pair_offset)
    hbm = pl.BlockSpec(memory_space=pltpu.HBM)
    anywhere = pl.BlockSpec(memory_space=pl.ANY)
    dma = pltpu.SemaphoreType.DMA
    field = pl.pallas_call(
        functools.partial(kernel, n_orb, n_pair, fold),
        out_shape=jax.ShapeDtypeStruct((owned * own_rows, plane), bf16),
        in_specs=[hbm] * 4,
        out_specs=anywhere,
        scratch_shapes=[
            pltpu.VMEM((owned, box_side, fold * LANES), f32),
            pltpu.VMEM((2, owned, box_side, LANES), f32),
            pltpu.VMEM((3, 1, 1, slots), jnp.int32),
            pltpu.VMEM((fold, owned + 1, box_side, LANES), bf16),
            pltpu.VMEM((n_orb, owned + 1, box_side, LANES), bf16),
            pltpu.VMEM((fold * owned * box_side, 5 * LANES), f32),
            pltpu.VMEM((twin, lines, LANES), f32),
            pltpu.VMEM((n_orb * n_pair // twin, lines, LANES), f32),
            pltpu.VMEM((n_orb, fold * owned * box_side, owned * box_side), bf16),
            pltpu.VMEM((n_pair * fold, owned * own_rows, LANES), bf16),
            dma((3,)),
            dma,
            dma((n_orb,)),
            dma((twin,)),
            dma((twin,)),
            dma,
            dma,
            dma,
            dma,
        ],
        compiler_params=pltpu.CompilerParams(
            collective_id=0, has_side_effects=True, vmem_limit_bytes=16 << 20
        ),
        name="exchange",
    )(*(pltpu.with_memory_space_constraint(x, pltpu.HBM) for x in inputs))
    return field.astype(f32).reshape(owned, own_rows, plane)


def solution(mesh):
    n_orb, n_pair = mesh.shape["orb"], mesh.shape["pair"]
    return jax.shard_map(
        functools.partial(local, n_orb, n_pair),
        mesh=mesh,
        in_specs=(
            P("orb", None, None),
            P("orb", "pair", None),
            P("orb", "pair", None),
            P("orb", "pair", None),
        ),
        out_specs=P("orb", "pair", None),
        check_vma=False,
    )
```
